32 devices in a mesh: grp: 4 (over y, core), slab: 8 (over z, x).
Axes of the slice: x: 2, y: 2, z: 4, core: 2. Of those that a mesh axis runs over, the one named last changes fastest.
Arguments:
- velocity: float32 [3, 32, 144, 512], P(None, 'slab', None, 'grp'), may hold values from -6 to 6
- w_in: bfloat16 [27, 16, 3], replicated, may hold values from -0.625 to 0.625
- w_mid_a: bfloat16 [27, 16, 16], replicated, may hold values from -0.3125 to 0.3125
- w_mid_b: bfloat16 [27, 16, 16], replicated, may hold values from -0.3125 to 0.3125
- w_out: bfloat16 [27, 6, 16], replicated, may hold values from -0.3125 to 0.3125
Outputs:
- velocity_next: float32 [3, 32, 144, 512], P(None, 'slab', None, 'grp')
- stress: bfloat16 [6, 16, 72, 256], P(None, 'slab', 'grp')
- grad_in: float32 [27, 16, 3], replicated
- grad_mid_a: float32 [27, 16, 16], replicated
- grad_mid_b: float32 [27, 16, 16], replicated
- grad_out: float32 [27, 6, 16], replicated
The draws below stay inside these ranges and needn't reach their ends.
All inputs are finite; a program needn't handle non-finite values.
Results may differ from the reference program's by a relative error of at most 0.0071.
Values may be sent and summed in bfloat16 or wider, within the bound.
No kernel may reach another device: no remote copies, remote signals or barrier semaphores. Data moves between devices by JAX's collectives and lax.ppermute only.
A program may use at most 448 MiB of HBM per device.

```python
import jax
import jax.numpy as jnp
from jax import lax

C = 16
NY = 144
NX = 32
NZ = 512


def shard_levels(stream_key, extent, shards, least, largest):
    def one(axis_at, shards_of):
        heights = jax.random.uniform(jax.random.fold_in(jax.random.fold_in(stream_key, 6), axis_at), (shards_of,), jnp.float32, least / len(shards), largest / len(shards))
        return jnp.repeat(jnp.exp(heights), extent[axis_at] // shards_of).reshape((-1,) + (1,) * (len(extent) - axis_at - 1))

    level = one(*shards[0])
    for cut in shards[1:]:
        level = level * one(*cut)
    return level


def gaussian(rng, shape, scale, reach, cuts=(), kind=jnp.bfloat16):
    loudness = shard_levels(rng, shape, cuts, -0.22, 0.18) if cuts else 1.0
    array = jax.random.normal(rng, shape, jnp.float32) * scale * loudness
    return jnp.minimum(jnp.maximum(array, -reach), reach).astype(kind)


def setup_inputs(seed: int = 0) -> dict:
    keys = jax.random.split(jax.random.key(seed), 6)
    velocity = gaussian(keys[0], (3, NX, NY, NZ), 1.0, 6.0, ((1, 8), (3, 4)), jnp.float32)
    w_in = gaussian(keys[1], (27, C, 3), (27 * 3) ** -0.5, 0.625)
    w_mid_a = gaussian(keys[2], (27, C, C), (27 * C) ** -0.5, 0.3125)
    w_mid_b = gaussian(keys[3], (27, C, C), (27 * C) ** -0.5, 0.3125)
    w_out = gaussian(keys[4], (27, 6, C), (27 * C) ** -0.5, 0.3125)
    return dict(velocity=velocity, w_in=w_in, w_mid_a=w_mid_a, w_mid_b=w_mid_b, w_out=w_out)


step_size = 0.1
viscosity = 0.5
closure_weight = 4.0
pair_table = ((0, 3, 4), (3, 1, 5), (4, 5, 2))
stress_pairs = ((0, 0), (1, 1), (2, 2), (0, 1), (0, 2), (1, 2))

def gradient_along(padded, along):
    length = padded.shape[along] - 4

    def window_at(offset):
        return lax.slice_in_dim(padded, offset, offset + length, axis=along)
    return (window_at(0) - 8.0 * window_at(1) + 8.0 * window_at(3) - window_at(4)) / 12.0

def laplace_along(padded, along):
    length = padded.shape[along] - 4

    def window_at(offset):
        return lax.slice_in_dim(padded, offset, offset + length, axis=along)
    return (-window_at(0) + 16.0 * window_at(1) - 30.0 * window_at(2) + 16.0 * window_at(3) - window_at(4)) / 12.0

def wall_ghosts(interior):
    return jnp.pad(interior, ((0, 0), (0, 0), (2, 2), (0, 0)))

def stress_force(extended):
    inner_x = extended[:, :, :, 2:-2]
    inner_z = extended[:, 2:-2]
    walled = wall_ghosts(extended[:, 2:-2, :, 2:-2])
    components = []
    for along_x, along_y, along_z in pair_table:
        summed = gradient_along(inner_x[along_x:along_x + 1], 1)
        summed = summed + gradient_along(walled[along_y:along_y + 1], 2)
        summed = summed + gradient_along(inner_z[along_z:along_z + 1], 3)
        components.append(-closure_weight * summed)
    return jnp.concatenate(components, axis=0)

def tendency(extended, forcing):
    inner_x = extended[:, :, :, 2:-2]
    inner_z = extended[:, 2:-2]
    interior = extended[:, 2:-2, :, 2:-2]
    walled = wall_ghosts(interior)
    advect = interior[0:1] * gradient_along(inner_x, 1)
    advect = advect + interior[1:2] * gradient_along(walled, 2)
    advect = advect + interior[2:3] * gradient_along(inner_z, 3)
    diffuse = laplace_along(inner_x, 1) + laplace_along(walled, 2) + laplace_along(inner_z, 3)
    return -advect + viscosity * diffuse + forcing

def block_mean(field):
    comps, cells_x, cells_y, cells_z = field.shape
    return field.reshape(comps, cells_x // 2, 2, cells_y // 2, 2, cells_z // 2, 2).mean(axis=(2, 4, 6))

def filter_fields(velocity):
    block_means = block_mean(velocity)
    products = jnp.stack([velocity[left_comp] * velocity[right_comp] for left_comp, right_comp in stress_pairs])
    resolved = jnp.stack([block_means[left_comp] * block_means[right_comp] for left_comp, right_comp in stress_pairs])
    return jnp.concatenate([block_means, block_mean(products) - resolved], axis=0).astype(jnp.bfloat16)

def prolong(coarse):
    return jnp.repeat(jnp.repeat(jnp.repeat(coarse, 2, axis=1), 2, axis=2), 2, axis=3)

def convolve(activation, weight):
    out_ch, in_ch = (weight.shape[1], weight.shape[2])
    padded = jnp.pad(activation, ((0, 0), (1, 1), (0, 0), (1, 1)), mode='wrap')
    padded = jnp.pad(padded, ((0, 0), (0, 0), (1, 1), (0, 0)))
    kernel = weight.reshape(3, 3, 3, out_ch, in_ch).transpose(3, 4, 0, 1, 2)
    return lax.conv_general_dilated(padded[None], kernel, (1, 1, 1), 'VALID', precision=lax.Precision.HIGHEST)[0]

def periodic_rim(field, width):
    return jnp.pad(field, ((0, 0), (width, width), (0, 0), (width, width)), mode='wrap')

def reference(velocity, w_in, w_mid_a, w_mid_b, w_out):
    coarse = filter_fields(velocity).astype(jnp.float32)
    weights = [weight.astype(jnp.float32) for weight in (w_in, w_mid_a, w_mid_b, w_out)]
    activation = coarse[:3]
    inputs = []
    response = activation
    for layer_index in range(4):
        inputs.append(activation)
        response = convolve(activation, weights[layer_index])
        if layer_index < 3:
            activation = lax.optimization_barrier(jnp.tanh(response).astype(jnp.bfloat16)).astype(jnp.float32)
    predicted = response
    stress = predicted.astype(jnp.bfloat16)
    length = 6 * predicted.shape[1] * predicted.shape[2] * predicted.shape[3]
    cotangent = (2.0 / length * (predicted - coarse[3:])).astype(jnp.bfloat16)
    cotangent = lax.optimization_barrier(cotangent).astype(jnp.float32)
    gradients = [None, None, None, None]
    for layer_index in (3, 2, 1, 0):
        unused_out, pullback = jax.vjp(convolve, inputs[layer_index], weights[layer_index])
        spread, gradients[layer_index] = pullback(cotangent)
        if layer_index > 0:
            below_act = inputs[layer_index]
            cotangent = (spread * (1.0 - below_act * below_act)).astype(jnp.bfloat16)
            cotangent = lax.optimization_barrier(cotangent).astype(jnp.float32)
    extended_tau = prolong(periodic_rim(stress.astype(jnp.float32), 1))
    forcing = stress_force(extended_tau)
    first_section = velocity + step_size * tendency(periodic_rim(velocity, 2), forcing)
    second = tendency(periodic_rim(first_section, 2), forcing)
    velocity_next = 0.5 * (velocity + first_section + step_size * second)
    return (velocity_next, stress, gradients[0], gradients[1], gradients[2], gradients[3])
```

```python
import functools

import jax
import jax.numpy as jnp
import numpy as np
from jax import lax
from jax.experimental import pallas as pl
from jax.experimental.pallas import tpu as pltpu
from jax.sharding import PartitionSpec as P

step_size = 0.1
viscosity = 0.5
closure_weight = 4.0
pair_table = ((0, 3, 4), (3, 1, 5), (4, 5, 2))
stress_pairs = ((0, 0), (1, 1), (2, 2), (0, 1), (0, 2), (1, 2))
LAYERS = 4
CH = 16
MARGIN = LAYERS + LAYERS - 1
f32 = jnp.float32
bf16 = jnp.bfloat16
VMEM_LIMIT = 60 * 1024 * 1024


def round_up(a, b):
    return -(-a // b) * b


def log2(n):
    assert n & (n - 1) == 0
    return n.bit_length() - 1


def call(body, out_shape, scratch, cost, n_in):
    many = isinstance(out_shape, (tuple, list))
    spec = pl.BlockSpec(memory_space=pltpu.VMEM)
    return pl.pallas_call(
        body,
        out_shape=out_shape,
        in_specs=[spec] * n_in,
        out_specs=[spec] * len(out_shape) if many else spec,
        scratch_shapes=scratch,
        compiler_params=pltpu.CompilerParams(vmem_limit_bytes=VMEM_LIMIT),
        cost_estimate=pl.CostEstimate(flops=cost, bytes_accessed=cost // 400, transcendentals=0),
    )


def granule_swap(arrays):
    n = len(arrays)
    lanes = arrays[0].shape[1]
    gran = lanes // n
    granule = lax.broadcasted_iota(jnp.int32, arrays[0].shape, 1) >> log2(gran)
    arrays = list(arrays)
    hop = 1
    while hop < n:
        upper = (granule & hop) != 0
        for i in range(n):
            if i & hop:
                continue
            low, high = arrays[i], arrays[i + hop]
            arrays[i] = jnp.where(upper, pltpu.roll(high, hop * gran, 1), low)
            arrays[i + hop] = jnp.where(upper, high, pltpu.roll(low, lanes - hop * gran, 1))
        hop *= 2
    return arrays


def rounded(x):
    return x.astype(bf16).astype(f32)


def filter_kernel(n, v_ref, out_ref, q_ref, f_ref):
    comps, fine_x, fine_y, fine_z = v_ref.shape
    cx, cy, cz = fine_x // 2, fine_y // 2, fine_z // 2
    zl = cz // n
    group = out_ref.shape[1]
    lanes = out_ref.shape[2]

    def chunk(j, carry):
        for xi in range(cx):
            sums = [None] * 9
            for a in range(2):
                for p in range(2):
                    cell = [v_ref[c, 2 * xi + a, pl.ds(16 * j + p, 8, stride=2), :] for c in range(3)]
                    terms = cell + [cell[l] * cell[r] for l, r in stress_pairs]
                    sums = [t if s is None else s + t for s, t in zip(sums, terms)]
            for k in range(9):
                q_ref[pl.ds(pl.multiple_of(k * cy + 8 * j, 8), 8), xi * fine_z : (xi + 1) * fine_z] = sums[k]
        return carry

    lax.fori_loop(0, cy // 8, chunk, 0)
    row = lax.broadcasted_iota(jnp.int32, (cx * fine_z, lanes), 0)
    col = lax.broadcasted_iota(jnp.int32, (cx * fine_z, lanes), 1)
    row_x = row >> log2(fine_z)
    row_z = (row & (fine_z - 1)) >> 1
    col_x = (col & (cx * zl - 1)) >> log2(zl)
    col_z = (col >> log2(cx * zl)) * zl + (col & (zl - 1))
    proj = jnp.where((row_x == col_x) & (row_z == col_z), 0.125, 0.0).astype(f32)
    means = []
    for k in range(9):
        mean = jnp.dot(
            q_ref[k * cy : (k + 1) * cy, :],
            proj,
            precision=lax.Precision.HIGHEST,
            preferred_element_type=f32,
        )
        if k < 3:
            means.append(mean)
        else:
            l, r = stress_pairs[k - 3]
            mean = mean - means[l] * means[r]
        f_ref[k * cy : (k + 1) * cy, :] = mean
    tail = n * group - 9 * cy
    if tail:
        f_ref[9 * cy :, :] = jnp.zeros((tail, lanes), f32)

    def swap(j, carry):
        base = pl.multiple_of(16 * j, 16)
        parts = granule_swap([f_ref[pl.ds(r * group + base, 16), :] for r in range(n)])
        for d in range(n):
            out_ref[d, pl.ds(base, 16), :] = parts[d].astype(bf16)
        return carry

    lax.fori_loop(0, group // 16, swap, 0)


def edge_kernel(v_ref, v16_ref, e_ref):
    comps, fine_x, fine_y, fine_z = v_ref.shape
    row = lax.broadcasted_iota(jnp.int32, (fine_z, 128), 0)
    col = lax.broadcasted_iota(jnp.int32, (fine_z, 128), 1)
    total = jnp.zeros((fine_y, 128), f32)
    for c in range(comps):
        for x in range(fine_x):
            block = v_ref[c, x].astype(bf16)
            base = (c * fine_x + x) * 8
            v16_ref[(c * fine_x + x) * fine_y : (c * fine_x + x + 1) * fine_y, :] = block
            e = col - base
            hit = ((e >= 0) & (e < 4) & (row == e)) | ((e >= 4) & (e < 8) & (row == fine_z - 8 + e))
            total = total + jnp.dot(
                block, jnp.where(hit, 1.0, 0.0).astype(bf16), preferred_element_type=f32
            )
    e_ref[...] = total.astype(bf16)


def closure_kernel(dims, *refs):
    n, hops, groups, devices, cy, cx, zl, length = dims
    nt = 2 * hops + 1
    tiles = refs[:nt]
    wf_ref, wb_ref, idx_ref = refs[nt : nt + 3]
    bsend_ref, ssend_ref, grad_ref = refs[nt + 3 : nt + 6]
    acts = refs[nt + 6 : nt + 10]
    cot_ref, cz_ref, f_ref, fs_ref, g_ref = refs[nt + 10 :]
    group = tiles[0].shape[1]
    lanes = tiles[0].shape[2]
    own = hops * lanes
    zpos = lax.broadcasted_iota(jnp.int32, (CH, lanes), 1) & (zl - 1)
    first_z = zpos == 0
    last_z = zpos == zl - 1

    def tile(value, t):
        t = min(max(t, 0), nt - 1)
        return value[:, t * lanes : (t + 1) * lanes]

    def after(value, t):
        return jnp.where(
            last_z, pltpu.roll(tile(value, t + 1), zl - 1, 1), pltpu.roll(tile(value, t), lanes - 1, 1)
        )

    def before(value, t):
        return jnp.where(
            first_z,
            pltpu.roll(tile(value, t - 1), lanes - (zl - 1), 1),
            pltpu.roll(tile(value, t), 1, 1),
        )

    def put(ref, y, value):
        for t in range(nt):
            v = tile(value, t)
            at = slice(t * lanes, (t + 1) * lanes)
            ref[y + 1, 0:CH, at] = pltpu.roll(v, zl, 1).astype(bf16)
            ref[y + 1, CH : 2 * CH, at] = v.astype(bf16)
            ref[y + 1, 2 * CH : 3 * CH, at] = pltpu.roll(v, lanes - zl, 1).astype(bf16)

    def put_cz(y, value):
        value = rounded(value)
        cz_ref[y, 0:CH, :] = after(value, hops).astype(bf16)
        cz_ref[y, CH : 2 * CH, :] = tile(value, hops).astype(bf16)
        cz_ref[y, 2 * CH : 3 * CH, :] = before(value, hops).astype(bf16)

    def convolve(src, w, y):
        columns = src[pl.ds(y, 3)].reshape(9 * CH, nt * lanes)
        parts = jnp.dot(w, columns, preferred_element_type=f32)
        low, mid, high = parts[0:CH], parts[CH : 2 * CH], parts[2 * CH :]
        return jnp.concatenate(
            [tile(mid, t) + before(low, t) + after(high, t) for t in range(nt)], axis=1
        )

    for ref in (*acts, cot_ref):
        zero = jnp.zeros((3 * CH, nt * lanes), bf16)
        ref[0] = zero
        ref[cy + 1] = zero
    for t in range(nt):
        used = n * group
        if used < CH * cy:
            f_ref[t, used:, :] = jnp.zeros((CH * cy - used, lanes), f32)

        def swap(j, carry, t=t):
            base = pl.multiple_of(16 * j, 16)
            parts = granule_swap([tiles[t][s, pl.ds(base, 16), :].astype(f32) for s in range(n)])
            for r in range(n):
                f_ref[t, pl.ds(r * group + base, 16), :] = parts[r]
            return carry

        lax.fori_loop(0, group // 16, swap, 0)

    def load_fields(y):
        return jnp.concatenate([f_ref[t, pl.ds(y, CH, stride=cy), :] for t in range(nt)], axis=1)

    def start(y, carry):
        put(acts[0], y, load_fields(y))
        return carry

    lax.fori_loop(0, cy, start, 0)

    for k in range(LAYERS - 1):
        w = wf_ref[k]

        def forward(y, carry, k=k, w=w):
            put(acts[k + 1], y, jnp.tanh(convolve(acts[k], w, y)))
            return carry

        lax.fori_loop(0, cy, forward, 0)

    w_last = wf_ref[LAYERS - 1]
    channel = lax.broadcasted_iota(jnp.int32, (CH, nt * lanes), 0)
    stressed = (channel >= 3) & (channel < 9)

    def predict(y, carry):
        predicted = convolve(acts[LAYERS - 1], w_last, y)
        target = load_fields(y)
        cot = jnp.where(stressed, 2.0 / length * (predicted - target), 0.0)
        put(cot_ref, y, cot)
        put_cz(y, cot)
        stress = rounded(predicted)
        for t in range(nt):
            f_ref[t, pl.ds(y, CH, stride=cy), :] = tile(stress, t)
        return carry

    lax.fori_loop(0, cy, predict, 0)

    def weight_gradient(src, k):
        def pair(j, acc):
            y = 2 * j
            left = jnp.concatenate([cz_ref[y], cz_ref[y + 1]], axis=1)
            right = jnp.concatenate(
                [
                    src[pl.ds(y, 3), :, own : own + lanes].reshape(9 * CH, lanes),
                    src[pl.ds(y + 1, 3), :, own : own + lanes].reshape(9 * CH, lanes),
                ],
                axis=1,
            )
            return acc + lax.dot_general(
                left, right, (((1,), (1,)), ((), ())), preferred_element_type=f32
            )

        g_ref[k] = lax.fori_loop(0, cy // 2, pair, jnp.zeros((3 * CH, 9 * CH), f32))

    weight_gradient(acts[LAYERS - 1], LAYERS - 1)
    source = cot_ref
    for k in range(LAYERS - 1, 0, -1):
        w = wb_ref[k]
        here = acts[k]

        def backward(y, carry, w=w, here=here, source=source, k=k):
            spread = convolve(source, w, y)
            below = here[y + 1, CH : 2 * CH, :].astype(f32)
            cot = spread * (1.0 - below * below)
            if k > 1:
                put(here, y, cot)
            put_cz(y, cot)
            return carry

        lax.fori_loop(0, cy, backward, 0)
        weight_gradient(acts[k - 1], k - 1)
        source = here

    rows = LAYERS * 3 * CH
    main = 8 * CH
    rest = jnp.zeros((rows // 8, main), f32)
    for k in range(LAYERS):
        grad_ref[k * 3 * CH : (k + 1) * 3 * CH, :] = g_ref[k, :, 0:main]
        for half in range(2):
            j = 2 * k + half
            piece = g_ref[k, half * 24 : half * 24 + 24, main:]
            piece = jnp.concatenate([piece, jnp.zeros((24, main - CH), f32)], axis=1)
            rest = rest + (pltpu.roll(piece, j * CH, 1) if j else piece)
    grad_ref[rows : rows + rows // 8, :] = rest
    if grad_ref.shape[0] > rows + rows // 8:
        grad_ref[rows + rows // 8 :, :] = jnp.zeros(
            (grad_ref.shape[0] - rows - rows // 8, main), f32
        )

    left = jnp.concatenate(
        [
            f_ref[t, (3 + 3 * half) * cy : (6 + 3 * half) * cy, :].astype(bf16)
            for half in range(2)
            for t in range(nt)
        ],
        axis=1,
    )
    row = lax.broadcasted_iota(jnp.int32, (2 * nt * lanes, 256), 0)
    for d in range(n // 2):
        pick = jnp.where(row == idx_ref[d], 1.0, 0.0).astype(bf16)
        moved = jnp.dot(left, pick, preferred_element_type=f32).astype(bf16)
        bsend_ref[2 * d] = moved[:, 0:128]
        bsend_ref[2 * d + 1] = moved[:, 128:256]

    wide = cy // groups
    srows = ssend_ref.shape[1]
    fs_ref[...] = jnp.zeros(fs_ref.shape, f32)
    for g in range(groups):
        for c in range(6):
            at = (3 + c) * cy + g * wide
            fs_ref[c * wide : (c + 1) * wide, :] = f_ref[hops, at : at + wide, :]
        for j in range(srows // 16):
            parts = granule_swap(
                [fs_ref[r * srows + 16 * j : r * srows + 16 * j + 16, :] for r in range(n)]
            )
            for d in range(n):
                ssend_ref[g * n + d, 16 * j : 16 * j + 16, :] = parts[d].astype(bf16)


def stress_kernel(n, groups, zl, recv_ref, out_ref, fs_ref):
    comps, cx, wide, depth = out_ref.shape
    srows = recv_ref.shape[1]
    lanes = recv_ref.shape[2]
    cz = n * zl
    for g in range(groups):
        for j in range(srows // 16):
            parts = granule_swap(
                [recv_ref[g * n + s, 16 * j : 16 * j + 16, :].astype(f32) for s in range(n)]
            )
            for r in range(n):
                fs_ref[g, r * srows + 16 * j : r * srows + 16 * j + 16, :] = parts[r]
    row = lax.broadcasted_iota(jnp.int32, (2 * lanes, 2 * cz), 0)
    col = lax.broadcasted_iota(jnp.int32, (2 * lanes, 2 * cz), 1)
    z = col & (cz - 1)
    need = (col >> log2(cz)) * lanes + (z >> log2(zl)) * (cx * zl) + (z & (zl - 1))
    used = round_up(comps * wide, 8)
    for xi in range(cx):
        pick = jnp.where(row == need + xi * zl, 1.0, 0.0).astype(bf16)
        for pair in range(groups // 2):
            left = jnp.concatenate(
                [fs_ref[2 * pair, 0:used, :], fs_ref[2 * pair + 1, 0:used, :]], axis=1
            ).astype(bf16)
            moved = jnp.dot(left, pick, preferred_element_type=f32)
            for c in range(comps):
                out_ref[c, xi, :, 2 * cz * pair : 2 * cz * (pair + 1)] = moved[
                    c * wide : (c + 1) * wide
                ].astype(bf16)


def unpack_kernel(all_ref, in_ref, mid_a_ref, mid_b_ref, out_ref):
    rows = LAYERS * 3 * CH
    main = 8 * CH
    rest = all_ref[rows : rows + rows // 8, :]
    for k, (ref, first, count, inputs) in enumerate(
        ((in_ref, 0, CH, 3), (mid_a_ref, 0, CH, CH), (mid_b_ref, 0, CH, CH), (out_ref, 3, 6, CH))
    ):
        block = all_ref[k * 3 * CH : (k + 1) * 3 * CH, :]
        tails = []
        for half in range(2):
            j = 2 * k + half
            tails.append(pltpu.roll(rest, main - j * CH, 1) if j else rest)
        tail = jnp.concatenate(tails, axis=0)
        for dy in range(3):
            for dx in range(3):
                at = dy * 3 + dx
                if at == 8:
                    moved = tail
                else:
                    moved = pltpu.roll(block, main - at * CH, 1) if at else block
                for dz in range(3):
                    ref[(dx * 3 + dy) * 3 + dz] = moved[
                        dz * CH + first : dz * CH + first + count, 0:inputs
                    ]


def tendency(ref, x, y0, rows, forcing):
    wide = ref.shape[-1]

    def at(c, dx, dy):
        return ref[c, x + dx, y0 + 8 + dy : y0 + 8 + dy + rows, :]

    centre = [at(c, 0, 0) for c in range(3)]
    results = []
    for i in range(3):
        f0 = centre[i]
        total = None
        for j in range(3):
            if j == 0:
                m2, m1, p1, p2 = (at(i, k, 0) for k in (-2, -1, 1, 2))
            elif j == 1:
                m2, m1, p1, p2 = (at(i, 0, k) for k in (-2, -1, 1, 2))
            else:
                m2, m1, p1, p2 = (pltpu.roll(f0, (-k) % wide, 1) for k in (-2, -1, 1, 2))
            slope = 8.0 * (p1 - m1) - (p2 - m2)
            curve = 16.0 * (p1 + m1) - (p2 + m2) - 30.0 * f0
            term = viscosity * curve - centre[j] * slope
            total = term if total is None else total + term
        results.append((f0, total / 12.0 + forcing[i]))
    return results


def advance_kernel(n, v_ref, ez_ref, xl_ref, xr_ref, st_ref, idx_ref, out_ref, u_ref, f1_ref, t_ref, frc_ref):
    comps, fine_x, fine_y, fine_z = v_ref.shape
    cy = fine_y // 2
    wide = 2 * fine_z
    pad = jnp.zeros((8, wide), f32)
    rows_v = comps * fine_x * fine_y
    for c in range(comps):
        for x in range(3 * fine_x):
            u_ref[c, x, 0:8, :] = pad
            u_ref[c, x, fine_y + 8 : fine_y + 16, :] = pad
        for x in range(fine_x):
            at = slice((c * fine_x + x) * fine_y, (c * fine_x + x + 1) * fine_y)
            u_ref[c, x, 8 : fine_y + 8, 0:fine_z] = xl_ref[at, :].astype(f32)
            u_ref[c, fine_x + x, 8 : fine_y + 8, 0:fine_z] = v_ref[c, x]
            u_ref[c, 2 * fine_x + x, 8 : fine_y + 8, 0:fine_z] = xr_ref[at, :].astype(f32)
        for x in range(2 * fine_x):
            f1_ref[c, x, 0:8, :] = pad
            f1_ref[c, x, fine_y + 8 : fine_y + 16, :] = pad
    edges = jnp.concatenate(
        [
            jnp.concatenate([ref[at : at + fine_y, :], ref[at + fine_y : at + 2 * fine_y, :]], axis=1)
            for ref, at in ((xl_ref, rows_v), (ez_ref, 0), (xr_ref, rows_v))
        ],
        axis=0,
    )
    row = lax.broadcasted_iota(jnp.int32, (256, 2 * fine_z), 0)
    col = lax.broadcasted_iota(jnp.int32, (256, 2 * fine_z), 1)
    lane = col & (fine_z - 1)
    for c in range(comps):
        for x in range(0, fine_x, 2):
            base = (c * fine_x + x) * 8 + (col >> log2(fine_z)) * 8
            need = jnp.where(lane < 4, 128 + base + lane, base + lane - (fine_z - 8))
            hit = (row == need) & ((lane < 4) | (lane >= fine_z - 4))
            moved = jnp.dot(
                edges, jnp.where(hit, 1.0, 0.0).astype(bf16), preferred_element_type=f32
            )
            for s in range(3):
                for e in range(2):
                    u_ref[c, s * fine_x + x + e, 8 : fine_y + 8, fine_z:wide] = moved[
                        s * fine_y : (s + 1) * fine_y, e * fine_z : (e + 1) * fine_z
                    ]

    half_lane = lax.broadcasted_iota(jnp.int32, (3 * cy, 128), 1) < 64
    lows, highs = [], []
    for s in range(0, n, 2):
        a, b = st_ref[s].astype(f32), st_ref[s + 1].astype(f32)
        lows.append(jnp.where(half_lane, a, pltpu.roll(b, 64, 1)).astype(bf16))
        highs.append(jnp.where(half_lane, pltpu.roll(a, 64, 1), b).astype(bf16))
    low = jnp.concatenate(lows, axis=1)
    high = jnp.concatenate(highs, axis=1)
    row = lax.broadcasted_iota(jnp.int32, (64 * n, wide), 0)
    for k in range(6):
        pick = jnp.where(row == idx_ref[k], 1.0, 0.0).astype(bf16)
        for h, src in enumerate((low, high)):
            moved = jnp.dot(src, pick, preferred_element_type=f32)
            for c in range(3):
                t_ref[3 * h + c, k, 0:8, :] = pad
                t_ref[3 * h + c, k, cy + 8 : cy + 16, :] = pad
                t_ref[3 * h + c, k, 8 : cy + 8, :] = moved[c * cy : (c + 1) * cy]

    scale = -closure_weight / 12.0

    def force(kk, carry):
        k = kk + 1
        for y0 in range(0, cy, 8):
            for i in range(3):
                ax, ay, az = pair_table[i]
                tz = t_ref[az, k, y0 + 8 : y0 + 16, :]
                m2, m1, p1, p2 = (pltpu.roll(tz, (-e) % wide, 1) for e in (-2, -1, 1, 2))
                along_z = 8.0 * (p1 - m1) - (p2 - m2)
                m, o, p = (t_ref[ay, k, y0 + 8 + e : y0 + 16 + e, :] for e in (-1, 0, 1))
                even = along_z + (8.0 * o - 7.0 * m - p)
                odd = along_z + (7.0 * p - 8.0 * o + m)
                m, o, p = (t_ref[ax, k + e, y0 + 8 : y0 + 16, :] for e in (-1, 0, 1))
                for px in range(2):
                    along_x = 7.0 * p - 8.0 * o + m if px else 8.0 * o - 7.0 * m - p
                    for py, part in enumerate((even, odd)):
                        value = scale * (along_x + part)
                        for h in range(0, wide, 128):
                            frc_ref[
                                h // 128, i, 2 * kk + px, pl.ds(2 * y0 + py, 8, stride=2), :
                            ] = value[:, h : h + 128]
        return carry

    lax.fori_loop(0, fine_x, force, 0)

    def forcing_at(x, y0):
        return [
            jnp.concatenate(
                [frc_ref[h, i, x, y0 : y0 + rows, :] for h in range(wide // 128)], axis=1
            )
            for i in range(3)
        ]

    rows = 8

    def one(x, carry):
        for y0 in range(0, fine_y, rows):
            for i, (f0, t) in enumerate(tendency(u_ref, x + 2, y0, rows, forcing_at(x, y0))):
                f1_ref[i, x, y0 + 8 : y0 + 8 + rows, :] = f0 + step_size * t
        return carry

    lax.fori_loop(0, 2 * fine_x, one, 0)

    def two(x, carry):
        for y0 in range(0, fine_y, rows):
            for i, (f0, t) in enumerate(tendency(f1_ref, x + 2, y0, rows, forcing_at(x + 2, y0))):
                nxt = (f0 + step_size * t)[:, 0:fine_z]
                out_ref[i, x, y0 : y0 + rows, :] = 0.5 * (v_ref[i, x, y0 : y0 + rows, :] + nxt)
        return carry

    lax.fori_loop(0, fine_x, two, 0)


def send_table(n, hops, cx, zl, lanes):
    nt = 2 * hops + 1
    total_x = n * cx
    window = zl + 2
    table = np.full((2, n // 2, 1, 256), -1, np.int32)
    for variant in range(2):
        z0 = -2 if variant == 0 else 0
        for d in range(n):
            for half in range(2):
                for xk in range(cx + 4):
                    for e in range(window):
                        x = (cx * d - 2 + xk) % total_x
                        z = z0 + e
                        t, zp = hops + z // zl, z % zl
                        src = half * nt * lanes + t * lanes + x * zl + zp
                        lane = half * 64 + xk * window + e
                        table[variant, d // 2, 0, (d % 2) * 128 + lane] = src
    return table


def spread_table(n, cx, zl, fine_z):
    window = zl + 2
    cz = fine_z // 2
    table = np.full((cx + 4, 1, 2 * fine_z), -1, np.int32)
    for k in range(cx + 4):
        for lane in range(2 * fine_z):
            if lane < fine_z + 4:
                z = lane // 2
            elif lane >= 2 * fine_z - 4:
                z = (lane - 2 * fine_z) // 2
            else:
                continue
            s = min(max(z // zl, 0), n - 1)
            z0 = -2 if s < n // 2 else 0
            table[k, 0, lane] = s * 64 + k * window + (z - s * zl - z0)
    return table


def local(velocity, w_in, w_mid_a, w_mid_b, w_out):
    n = lax.axis_size("slab")
    groups = lax.axis_size("grp")
    devices = n * groups
    comps, fine_x, fine_y, fine_z = velocity.shape
    cx, cy, cz = fine_x // 2, fine_y // 2, fine_z // 2
    zl = cz // n
    lanes = n * cx * zl
    hops = -(-MARGIN // zl)
    nt = 2 * hops + 1
    assert lanes == 128 and fine_z == 128 and cx == 2 and cy % 8 == 0 and (cx + 4) * (zl + 2) <= 64
    length = 6 * n * cx * cy * groups * cz
    both = ("grp", "slab")

    def ring(x, shift):
        return lax.ppermute(x, both, [(i, (i + shift) % devices) for i in range(devices)])

    def shift(x, axis, by):
        count = lax.axis_size(axis)
        return lax.ppermute(x, axis, [(i, (i + by) % count) for i in range(count)])

    spread = jnp.stack(
        [
            jnp.pad(w_in, ((0, 0), (0, 0), (0, CH - 3))),
            w_mid_a,
            w_mid_b,
            jnp.pad(w_out, ((0, 0), (3, CH - 9), (0, 0))),
        ]
    ).reshape(LAYERS, 3, 3, 3, CH, CH)
    w_fwd = jnp.transpose(spread, (0, 3, 4, 2, 1, 5)).reshape(LAYERS, 3 * CH, 9 * CH)
    w_bwd = jnp.transpose(spread[:, ::-1, ::-1, ::-1], (0, 3, 5, 2, 1, 4)).reshape(
        LAYERS, 3 * CH, 9 * CH
    )

    group = round_up(-(-9 * cy // n), 16)
    fields = call(
        functools.partial(filter_kernel, n),
        jax.ShapeDtypeStruct((n, group, lanes), bf16),
        [pltpu.VMEM((9 * cy, cx * fine_z), f32), pltpu.VMEM((n * group, lanes), f32)],
        4_000_000_000,
        1,
    )(velocity)
    mine = lax.all_to_all(fields, "slab", 0, 0, tiled=True)

    v16, edge = call(
        edge_kernel,
        (
            jax.ShapeDtypeStruct((comps * fine_x * fine_y, fine_z), bf16),
            jax.ShapeDtypeStruct((fine_y, 128), bf16),
        ),
        [],
        1_000_000_000,
        1,
    )(velocity)
    from_left = shift(edge, "grp", 1)
    from_right = shift(edge, "grp", -1)
    edges = jnp.concatenate([from_left, from_right], axis=0)

    lower = [ring(mine, k) for k in range(hops, 0, -1)]
    upper = [ring(mine, -k) for k in range(1, hops + 1)]
    edges, v16, lower, upper = lax.optimization_barrier((edges, v16, lower, upper))
    pack = jnp.concatenate([v16, edges], axis=0)
    pack_left = shift(pack, "slab", 1)
    pack_right = shift(pack, "slab", -1)

    place = lax.axis_index("slab")
    tables = send_table(n, hops, cx, zl, lanes)
    send_idx = jnp.where(place < n // 2, tables[0], tables[1])
    srows = round_up(-(-6 * (cy // groups) // n), 16)
    grad_rows = LAYERS * 3 * CH * 9 // 8
    per_device = round_up(-(-grad_rows // devices), 8)
    act = pltpu.VMEM((cy + 2, 3 * CH, nt * lanes), bf16)
    bsend, ssend, grads = call(
        functools.partial(
            closure_kernel, (n, hops, groups, devices, cy, cx, zl, length)
        ),
        (
            jax.ShapeDtypeStruct((n, 3 * cy, 128), bf16),
            jax.ShapeDtypeStruct((devices, srows, lanes), bf16),
            jax.ShapeDtypeStruct((devices * per_device, 128), f32),
        ),
        [
            act,
            act,
            act,
            act,
            act,
            pltpu.VMEM((cy, 3 * CH, lanes), bf16),
            pltpu.VMEM((nt, max(CH * cy, n * group), lanes), f32),
            pltpu.VMEM((n * srows, lanes), f32),
            pltpu.VMEM((LAYERS, 3 * CH, 9 * CH), f32),
        ],
        40_000_000_000,
        nt + 3,
    )(*lower, mine, *upper, w_fwd, w_bwd, send_idx)

    st = lax.all_to_all(bsend, "slab", 0, 0, tiled=True)
    partial_sums = lax.all_to_all(
        grads.reshape(devices, per_device, 128), both, 0, 0, tiled=True
    )
    total = jnp.sum(partial_sums, axis=0)
    summed = lax.all_to_all(
        jnp.broadcast_to(total[None], (devices, per_device, 128)), both, 0, 0, tiled=True
    ).reshape(devices * per_device, 128)
    out_blocks = lax.all_to_all(ssend, both, 0, 0, tiled=True)

    velocity_next = call(
        functools.partial(advance_kernel, n),
        jax.ShapeDtypeStruct(velocity.shape, f32),
        [
            pltpu.VMEM((comps, 3 * fine_x, fine_y + 16, 2 * fine_z), f32),
            pltpu.VMEM((comps, 2 * fine_x, fine_y + 16, 2 * fine_z), f32),
            pltpu.VMEM((6, cx + 4, cy + 16, 2 * fine_z), f32),
            pltpu.VMEM((2 * fine_z // 128, comps, 2 * fine_x, fine_y, 128), f32),
        ],
        15_000_000_000,
        6,
    )(velocity, edges, pack_left, pack_right, st, spread_table(n, cx, zl, fine_z))

    stress = call(
        functools.partial(stress_kernel, n, groups, zl),
        jax.ShapeDtypeStruct((6, cx, cy // groups, groups * cz), bf16),
        [pltpu.VMEM((groups, n * srows, lanes), f32)],
        1_000_000_000,
        1,
    )(out_blocks)
    grad_in, grad_mid_a, grad_mid_b, grad_out = call(
        unpack_kernel,
        (
            jax.ShapeDtypeStruct((27, CH, 3), f32),
            jax.ShapeDtypeStruct((27, CH, CH), f32),
            jax.ShapeDtypeStruct((27, CH, CH), f32),
            jax.ShapeDtypeStruct((27, 6, CH), f32),
        ),
        [],
        1_000_000_000,
        1,
    )(summed)
    return (velocity_next, stress, grad_in, grad_mid_a, grad_mid_b, grad_out)


def solution(mesh):
    in_specs = (P(None, "slab", None, "grp"), P(), P(), P(), P())
    out_specs = (P(None, "slab", None, "grp"), P(None, "slab", "grp", None), P(), P(), P(), P())
    return jax.shard_map(local, mesh=mesh, in_specs=in_specs, out_specs=out_specs, check_vma=False)
```

```python
import functools

import jax
import jax.numpy as jnp
import numpy as np
from jax import lax
from jax.experimental import pallas as pl
from jax.experimental.pallas import tpu as pltpu
from jax.sharding import PartitionSpec as P

step_size = 0.1
viscosity = 0.5
closure_weight = 4.0
pair_table = ((0, 3, 4), (3, 1, 5), (4, 5, 2))
stress_pairs = ((0, 0), (1, 1), (2, 2), (0, 1), (0, 2), (1, 2))
LAYERS = 4
CH = 16
MARGIN = LAYERS + LAYERS - 1
f32 = jnp.float32
bf16 = jnp.bfloat16
BATCH = 8
MIB = 1024 * 1024


def round_up(a, b):
    return -(-a // b) * b


def log2(n):
    assert n & (n - 1) == 0
    return n.bit_length() - 1


def nbytes(shapes):
    return sum(int(np.prod(x.shape)) * jnp.dtype(x.dtype).itemsize for x in shapes)


def call(body, out_shape, scratch, cost, n_in):
    many = isinstance(out_shape, (tuple, list))
    grant = max(36 * MIB, min(62 * MIB, int(1.1 * nbytes(scratch)) + 9 * MIB))
    spec = pl.BlockSpec(memory_space=pltpu.VMEM)
    return pl.pallas_call(
        body,
        out_shape=out_shape,
        in_specs=[spec] * n_in,
        out_specs=[spec] * len(out_shape) if many else spec,
        scratch_shapes=scratch,
        compiler_params=pltpu.CompilerParams(vmem_limit_bytes=grant),
        cost_estimate=pl.CostEstimate(flops=cost, bytes_accessed=cost // 400, transcendentals=0),
    )


def granule_swap(arrays):
    n = len(arrays)
    lanes = arrays[0].shape[1]
    gran = lanes // n
    granule = lax.broadcasted_iota(jnp.int32, arrays[0].shape, 1) >> log2(gran)
    arrays = list(arrays)
    hop = 1
    while hop < n:
        upper = (granule & hop) != 0
        for i in range(n):
            if i & hop:
                continue
            low, high = arrays[i], arrays[i + hop]
            arrays[i] = jnp.where(upper, pltpu.roll(high, hop * gran, 1), low)
            arrays[i + hop] = jnp.where(upper, high, pltpu.roll(low, lanes - hop * gran, 1))
        hop *= 2
    return arrays


def rounded(x):
    return x.astype(bf16).astype(f32)


def filter_kernel(n, v_ref, out_ref, q_ref, f_ref):
    _, fine_x, fine_y, fine_z = v_ref.shape
    cx, cy, cz = fine_x // 2, fine_y // 2, fine_z // 2
    zl = cz // n
    group = out_ref.shape[1]
    lanes = out_ref.shape[2]

    def chunk(j, carry):
        for xi in range(cx):
            sums = [None] * 9
            for a in range(2):
                for p in range(2):
                    cell = [v_ref[c, 2 * xi + a, pl.ds(16 * j + p, 8, stride=2), :] for c in range(3)]
                    terms = cell + [cell[l] * cell[r] for l, r in stress_pairs]
                    sums = [t if s is None else s + t for s, t in zip(sums, terms)]
            for k in range(9):
                q_ref[pl.ds(pl.multiple_of(k * cy + 8 * j, 8), 8), xi * fine_z : (xi + 1) * fine_z] = sums[k]
        return carry

    lax.fori_loop(0, cy // 8, chunk, 0)
    row = lax.broadcasted_iota(jnp.int32, (cx * fine_z, lanes), 0)
    col = lax.broadcasted_iota(jnp.int32, (cx * fine_z, lanes), 1)
    row_x = row >> log2(fine_z)
    row_z = (row & (fine_z - 1)) >> 1
    col_x = (col & (cx * zl - 1)) >> log2(zl)
    col_z = (col >> log2(cx * zl)) * zl + (col & (zl - 1))
    proj = jnp.where((row_x == col_x) & (row_z == col_z), 0.125, 0.0).astype(f32)
    means = []
    for k in range(9):
        mean = jnp.dot(
            q_ref[k * cy : (k + 1) * cy, :],
            proj,
            precision=lax.Precision.HIGHEST,
            preferred_element_type=f32,
        )
        if k < 3:
            means.append(mean)
        else:
            l, r = stress_pairs[k - 3]
            mean = mean - means[l] * means[r]
        f_ref[k * cy : (k + 1) * cy, :] = mean
    tail = n * group - 9 * cy
    if tail:
        f_ref[9 * cy :, :] = jnp.zeros((tail, lanes), f32)

    def swap(j, carry):
        base = pl.multiple_of(16 * j, 16)
        parts = granule_swap([f_ref[pl.ds(r * group + base, 16), :] for r in range(n)])
        for d in range(n):
            out_ref[d, pl.ds(base, 16), :] = parts[d].astype(bf16)
        return carry

    lax.fori_loop(0, group // 16, swap, 0)


def edge_kernel(v_ref, v16_ref, e_ref):
    comps, fine_x, fine_y, fine_z = v_ref.shape
    row = lax.broadcasted_iota(jnp.int32, (fine_z, 128), 0)
    col = lax.broadcasted_iota(jnp.int32, (fine_z, 128), 1)
    total = jnp.zeros((fine_y, 128), f32)
    for c in range(comps):
        for x in range(fine_x):
            block = v_ref[c, x].astype(bf16)
            base = (c * fine_x + x) * 8
            v16_ref[(c * fine_x + x) * fine_y : (c * fine_x + x + 1) * fine_y, :] = block
            e = col - base
            hit = ((e >= 0) & (e < 4) & (row == e)) | ((e >= 4) & (e < 8) & (row == fine_z - 8 + e))
            total = total + jnp.dot(
                block, jnp.where(hit, 1.0, 0.0).astype(bf16), preferred_element_type=f32
            )
    e_ref[...] = total.astype(bf16)


def closure_kernel(dims, *refs):
    n, hops, groups, _, cy, _, zl, length = dims
    nt = 2 * hops + 1
    tiles = refs[:nt]
    wf_ref, wb_ref, idx_ref = refs[nt : nt + 3]
    bsend_ref, ssend_ref, grad_ref = refs[nt + 3 : nt + 6]
    acts = refs[nt + 6 : nt + 10]
    cot_ref, cz_ref, f_ref, fs_ref, g_ref = refs[nt + 10 :]
    unroll = max(u for u in range(1, cy + 1) if cy % u == 0 and u * nt <= 36)
    group = tiles[0].shape[1]
    lanes = tiles[0].shape[2]
    own = hops * lanes
    zpos = lax.broadcasted_iota(jnp.int32, (CH, lanes), 1) & (zl - 1)
    first_z = zpos == 0
    last_z = zpos == zl - 1

    def tile(value, t):
        t = min(max(t, 0), nt - 1)
        return value[:, t * lanes : (t + 1) * lanes]

    def after(value, t):
        return jnp.where(
            last_z, pltpu.roll(tile(value, t + 1), zl - 1, 1), pltpu.roll(tile(value, t), lanes - 1, 1)
        )

    def before(value, t):
        return jnp.where(
            first_z,
            pltpu.roll(tile(value, t - 1), lanes - (zl - 1), 1),
            pltpu.roll(tile(value, t), 1, 1),
        )

    def put(ref, y, value):
        for t in range(nt):
            v = tile(value, t)
            at = slice(t * lanes, (t + 1) * lanes)
            ref[y + 1, 0:CH, at] = pltpu.roll(v, zl, 1).astype(bf16)
            ref[y + 1, CH : 2 * CH, at] = v.astype(bf16)
            ref[y + 1, 2 * CH : 3 * CH, at] = pltpu.roll(v, lanes - zl, 1).astype(bf16)

    def put_cz(y, value):
        value = rounded(value)
        cz_ref[y, 0:CH, :] = after(value, hops).astype(bf16)
        cz_ref[y, CH : 2 * CH, :] = tile(value, hops).astype(bf16)
        cz_ref[y, 2 * CH : 3 * CH, :] = before(value, hops).astype(bf16)

    def convolve(src, w, ys):
        results = []
        for y in ys:
            columns = src[pl.ds(y, 3)].reshape(9 * CH, nt * lanes)
            results.append(jnp.dot(w, columns, preferred_element_type=f32))
        sums = []
        for parts in results:
            low, mid, high = parts[0:CH], parts[CH : 2 * CH], parts[2 * CH :]
            sums.append(
                jnp.concatenate(
                    [tile(mid, t) + before(low, t) + after(high, t) for t in range(nt)], axis=1
                )
            )
        return sums

    def rows_at(j):
        return [unroll * j + u for u in range(unroll)]

    for ref in (*acts, cot_ref):
        zero = jnp.zeros((3 * CH, nt * lanes), bf16)
        ref[0] = zero
        ref[cy + 1] = zero
    for t in range(nt):
        used = n * group
        if used < CH * cy:
            f_ref[t, used:, :] = jnp.zeros((CH * cy - used, lanes), f32)

        def swap(j, carry, t=t):
            base = pl.multiple_of(16 * j, 16)
            parts = granule_swap([tiles[t][s, pl.ds(base, 16), :].astype(f32) for s in range(n)])
            for r in range(n):
                f_ref[t, pl.ds(r * group + base, 16), :] = parts[r]
            return carry

        lax.fori_loop(0, group // 16, swap, 0)

    def load_fields(y):
        return jnp.concatenate([f_ref[t, pl.ds(y, CH, stride=cy), :] for t in range(nt)], axis=1)

    def start(j, carry):
        for y in rows_at(j):
            put(acts[0], y, load_fields(y))
        return carry

    lax.fori_loop(0, cy // unroll, start, 0)

    for k in range(LAYERS - 1):
        w = wf_ref[k]

        def forward(j, carry, k=k, w=w):
            ys = rows_at(j)
            outs = [jnp.tanh(v) for v in convolve(acts[k], w, ys)]
            for y, v in zip(ys, outs):
                put(acts[k + 1], y, v)
            return carry

        lax.fori_loop(0, cy // unroll, forward, 0)

    w_last = wf_ref[LAYERS - 1]
    channel = lax.broadcasted_iota(jnp.int32, (CH, nt * lanes), 0)
    stressed = (channel >= 3) & (channel < 9)

    def predict(j, carry):
        ys = rows_at(j)
        targets = [load_fields(y) for y in ys]
        predicted = convolve(acts[LAYERS - 1], w_last, ys)
        cots = [
            jnp.where(stressed, 2.0 / length * (v - target), 0.0)
            for v, target in zip(predicted, targets)
        ]
        for y, cot in zip(ys, cots):
            put(cot_ref, y, cot)
            put_cz(y, cot)
        for y, v in zip(ys, predicted):
            stress = rounded(v)
            for t in range(nt):
                f_ref[t, pl.ds(y, CH, stride=cy), :] = tile(stress, t)
        return carry

    lax.fori_loop(0, cy // unroll, predict, 0)

    def weight_gradient(src, k):
        def pair(j, acc):
            ys = [BATCH * j + u for u in range(BATCH)]
            left = jnp.concatenate([cz_ref[y] for y in ys], axis=1)
            right = jnp.concatenate(
                [src[pl.ds(y, 3), :, own : own + lanes].reshape(9 * CH, lanes) for y in ys],
                axis=1,
            )
            return acc + lax.dot_general(
                left, right, (((1,), (1,)), ((), ())), preferred_element_type=f32
            )

        g_ref[k] = lax.fori_loop(0, cy // BATCH, pair, jnp.zeros((3 * CH, 9 * CH), f32))

    weight_gradient(acts[LAYERS - 1], LAYERS - 1)
    source = cot_ref
    for k in range(LAYERS - 1, 0, -1):
        w = wb_ref[k]
        here = acts[k]

        def backward(j, carry, w=w, here=here, source=source, k=k):
            ys = rows_at(j)
            below = [here[y + 1, CH : 2 * CH, :].astype(f32) for y in ys]
            cots = [v * (1.0 - b * b) for v, b in zip(convolve(source, w, ys), below)]
            for y, cot in zip(ys, cots):
                if k > 1:
                    put(here, y, cot)
                put_cz(y, cot)
            return carry

        lax.fori_loop(0, cy // unroll, backward, 0)
        weight_gradient(acts[k - 1], k - 1)
        source = here

    rows = LAYERS * 3 * CH
    main = 8 * CH
    rest = jnp.zeros((rows // 8, main), f32)
    for k in range(LAYERS):
        grad_ref[k * 3 * CH : (k + 1) * 3 * CH, :] = g_ref[k, :, 0:main]
        for half in range(2):
            j = 2 * k + half
            piece = g_ref[k, half * 24 : half * 24 + 24, main:]
            piece = jnp.concatenate([piece, jnp.zeros((24, main - CH), f32)], axis=1)
            rest = rest + (pltpu.roll(piece, j * CH, 1) if j else piece)
    grad_ref[rows : rows + rows // 8, :] = rest
    if grad_ref.shape[0] > rows + rows // 8:
        grad_ref[rows + rows // 8 :, :] = jnp.zeros(
            (grad_ref.shape[0] - rows - rows // 8, main), f32
        )

    left = jnp.concatenate(
        [
            f_ref[t, (3 + 3 * half) * cy : (6 + 3 * half) * cy, :].astype(bf16)
            for half in range(2)
            for t in range(nt)
        ],
        axis=1,
    )
    row = lax.broadcasted_iota(jnp.int32, (2 * nt * lanes, 256), 0)
    for d in range(n // 2):
        pick = jnp.where(row == idx_ref[d], 1.0, 0.0).astype(bf16)
        moved = jnp.dot(left, pick, preferred_element_type=f32).astype(bf16)
        bsend_ref[2 * d] = moved[:, 0:128]
        bsend_ref[2 * d + 1] = moved[:, 128:256]

    wide = cy // groups
    srows = ssend_ref.shape[1]
    fs_ref[...] = jnp.zeros(fs_ref.shape, f32)
    for g in range(groups):
        for c in range(6):
            at = (3 + c) * cy + g * wide
            fs_ref[c * wide : (c + 1) * wide, :] = f_ref[hops, at : at + wide, :]
        for j in range(srows // 16):
            parts = granule_swap(
                [fs_ref[r * srows + 16 * j : r * srows + 16 * j + 16, :] for r in range(n)]
            )
            for d in range(n):
                ssend_ref[g * n + d, 16 * j : 16 * j + 16, :] = parts[d].astype(bf16)


def stress_kernel(n, groups, zl, recv_ref, out_ref, fs_ref):
    comps, cx, wide, _ = out_ref.shape
    srows = recv_ref.shape[1]
    lanes = recv_ref.shape[2]
    cz = n * zl
    for g in range(groups):
        for j in range(srows // 16):
            parts = granule_swap(
                [recv_ref[g * n + s, 16 * j : 16 * j + 16, :].astype(f32) for s in range(n)]
            )
            for r in range(n):
                fs_ref[g, r * srows + 16 * j : r * srows + 16 * j + 16, :] = parts[r]
    row = lax.broadcasted_iota(jnp.int32, (2 * lanes, 2 * cz), 0)
    col = lax.broadcasted_iota(jnp.int32, (2 * lanes, 2 * cz), 1)
    z = col & (cz - 1)
    need = (col >> log2(cz)) * lanes + (z >> log2(zl)) * (cx * zl) + (z & (zl - 1))
    used = round_up(comps * wide, 8)
    for xi in range(cx):
        pick = jnp.where(row == need + xi * zl, 1.0, 0.0).astype(bf16)
        for pair in range(groups // 2):
            left = jnp.concatenate(
                [fs_ref[2 * pair, 0:used, :], fs_ref[2 * pair + 1, 0:used, :]], axis=1
            ).astype(bf16)
            moved = jnp.dot(left, pick, preferred_element_type=f32)
            for c in range(comps):
                out_ref[c, xi, :, 2 * cz * pair : 2 * cz * (pair + 1)] = moved[
                    c * wide : (c + 1) * wide
                ].astype(bf16)


def unpack_kernel(all_ref, in_ref, mid_a_ref, mid_b_ref, out_ref):
    rows = LAYERS * 3 * CH
    main = 8 * CH
    rest = all_ref[rows : rows + rows // 8, :]
    for k, (ref, first, count, inputs) in enumerate(
        ((in_ref, 0, CH, 3), (mid_a_ref, 0, CH, CH), (mid_b_ref, 0, CH, CH), (out_ref, 3, 6, CH))
    ):
        block = all_ref[k * 3 * CH : (k + 1) * 3 * CH, :]
        tails = []
        for half in range(2):
            j = 2 * k + half
            tails.append(pltpu.roll(rest, main - j * CH, 1) if j else rest)
        tail = jnp.concatenate(tails, axis=0)
        for dy in range(3):
            for dx in range(3):
                at = dy * 3 + dx
                if at == 8:
                    moved = tail
                else:
                    moved = pltpu.roll(block, main - at * CH, 1) if at else block
                for dz in range(3):
                    ref[(dx * 3 + dy) * 3 + dz] = moved[
                        dz * CH + first : dz * CH + first + count, 0:inputs
                    ]


def tendency(ref, x, y0, rows, forcing):
    wide = ref.shape[-1]

    def at(c, dx, dy):
        return ref[c, x + dx, y0 + 8 + dy : y0 + 8 + dy + rows, :]

    centre = [at(c, 0, 0) for c in range(3)]
    results = []
    for i in range(3):
        f0 = centre[i]
        total = None
        for j in range(3):
            if j == 0:
                m2, m1, p1, p2 = (at(i, k, 0) for k in (-2, -1, 1, 2))
            elif j == 1:
                m2, m1, p1, p2 = (at(i, 0, k) for k in (-2, -1, 1, 2))
            else:
                m2, m1, p1, p2 = (pltpu.roll(f0, (-k) % wide, 1) for k in (-2, -1, 1, 2))
            slope = 8.0 * (p1 - m1) - (p2 - m2)
            curve = 16.0 * (p1 + m1) - (p2 + m2) - 30.0 * f0
            term = viscosity * curve - centre[j] * slope
            total = term if total is None else total + term
        results.append((f0, total / 12.0 + forcing[i]))
    return results


def advance_kernel(n, v_ref, ez_ref, xl_ref, xr_ref, st_ref, idx_ref, out_ref, u_ref, f1_ref, t_ref, frc_ref):
    comps, fine_x, fine_y, fine_z = v_ref.shape
    cy = fine_y // 2
    wide = 2 * fine_z
    pad = jnp.zeros((8, wide), f32)
    rows_v = comps * fine_x * fine_y
    for c in range(comps):
        for x in range(3 * fine_x):
            u_ref[c, x, 0:8, :] = pad
            u_ref[c, x, fine_y + 8 : fine_y + 16, :] = pad
        for x in range(fine_x):
            at = slice((c * fine_x + x) * fine_y, (c * fine_x + x + 1) * fine_y)
            u_ref[c, x, 8 : fine_y + 8, 0:fine_z] = xl_ref[at, :].astype(f32)
            u_ref[c, fine_x + x, 8 : fine_y + 8, 0:fine_z] = v_ref[c, x]
            u_ref[c, 2 * fine_x + x, 8 : fine_y + 8, 0:fine_z] = xr_ref[at, :].astype(f32)
        for x in range(2 * fine_x):
            f1_ref[c, x, 0:8, :] = pad
            f1_ref[c, x, fine_y + 8 : fine_y + 16, :] = pad
    edges = jnp.concatenate(
        [
            jnp.concatenate([ref[at : at + fine_y, :], ref[at + fine_y : at + 2 * fine_y, :]], axis=1)
            for ref, at in ((xl_ref, rows_v), (ez_ref, 0), (xr_ref, rows_v))
        ],
        axis=0,
    )
    row = lax.broadcasted_iota(jnp.int32, (256, 2 * fine_z), 0)
    col = lax.broadcasted_iota(jnp.int32, (256, 2 * fine_z), 1)
    lane = col & (fine_z - 1)
    for c in range(comps):
        for x in range(0, fine_x, 2):
            base = (c * fine_x + x) * 8 + (col >> log2(fine_z)) * 8
            need = jnp.where(lane < 4, 128 + base + lane, base + lane - (fine_z - 8))
            hit = (row == need) & ((lane < 4) | (lane >= fine_z - 4))
            moved = jnp.dot(
                edges, jnp.where(hit, 1.0, 0.0).astype(bf16), preferred_element_type=f32
            )
            for s in range(3):
                for e in range(2):
                    u_ref[c, s * fine_x + x + e, 8 : fine_y + 8, fine_z:wide] = moved[
                        s * fine_y : (s + 1) * fine_y, e * fine_z : (e + 1) * fine_z
                    ]

    half_lane = lax.broadcasted_iota(jnp.int32, (3 * cy, 128), 1) < 64
    lows, highs = [], []
    for s in range(0, n, 2):
        a, b = st_ref[s].astype(f32), st_ref[s + 1].astype(f32)
        lows.append(jnp.where(half_lane, a, pltpu.roll(b, 64, 1)).astype(bf16))
        highs.append(jnp.where(half_lane, pltpu.roll(a, 64, 1), b).astype(bf16))
    low = jnp.concatenate(lows, axis=1)
    high = jnp.concatenate(highs, axis=1)
    row = lax.broadcasted_iota(jnp.int32, (64 * n, wide), 0)
    for k in range(6):
        pick = jnp.where(row == idx_ref[k], 1.0, 0.0).astype(bf16)
        for h, src in enumerate((low, high)):
            moved = jnp.dot(src, pick, preferred_element_type=f32)
            for c in range(3):
                t_ref[3 * h + c, k, 0:8, :] = pad
                t_ref[3 * h + c, k, cy + 8 : cy + 16, :] = pad
                t_ref[3 * h + c, k, 8 : cy + 8, :] = moved[c * cy : (c + 1) * cy]

    scale = -closure_weight / 12.0

    def force(kk, carry):
        k = kk + 1
        for y0 in range(0, cy, 8):
            for i in range(3):
                ax, ay, az = pair_table[i]
                tz = t_ref[az, k, y0 + 8 : y0 + 16, :]
                m2, m1, p1, p2 = (pltpu.roll(tz, (-e) % wide, 1) for e in (-2, -1, 1, 2))
                along_z = 8.0 * (p1 - m1) - (p2 - m2)
                m, o, p = (t_ref[ay, k, y0 + 8 + e : y0 + 16 + e, :] for e in (-1, 0, 1))
                even = along_z + (8.0 * o - 7.0 * m - p)
                odd = along_z + (7.0 * p - 8.0 * o + m)
                m, o, p = (t_ref[ax, k + e, y0 + 8 : y0 + 16, :] for e in (-1, 0, 1))
                for px in range(2):
                    along_x = 7.0 * p - 8.0 * o + m if px else 8.0 * o - 7.0 * m - p
                    for py, part in enumerate((even, odd)):
                        value = scale * (along_x + part)
                        for h in range(0, wide, 128):
                            frc_ref[
                                h // 128, i, 2 * kk + px, pl.ds(2 * y0 + py, 8, stride=2), :
                            ] = value[:, h : h + 128]
        return carry

    lax.fori_loop(0, fine_x, force, 0)

    def forcing_at(x, y0):
        return [
            jnp.concatenate(
                [frc_ref[h, i, x, y0 : y0 + rows, :] for h in range(wide // 128)], axis=1
            )
            for i in range(3)
        ]

    rows = 8

    def one(x, carry):
        for y0 in range(0, fine_y, rows):
            for i, (f0, t) in enumerate(tendency(u_ref, x + 2, y0, rows, forcing_at(x, y0))):
                f1_ref[i, x, y0 + 8 : y0 + 8 + rows, :] = f0 + step_size * t
        return carry

    lax.fori_loop(0, 2 * fine_x, one, 0)

    def two(x, carry):
        for y0 in range(0, fine_y, rows):
            for i, (f0, t) in enumerate(tendency(f1_ref, x + 2, y0, rows, forcing_at(x + 2, y0))):
                nxt = (f0 + step_size * t)[:, 0:fine_z]
                out_ref[i, x, y0 : y0 + rows, :] = 0.5 * (v_ref[i, x, y0 : y0 + rows, :] + nxt)
        return carry

    lax.fori_loop(0, fine_x, two, 0)


def send_table(n, hops, cx, zl, lanes):
    nt = 2 * hops + 1
    total_x = n * cx
    window = zl + 2
    table = np.full((2, n // 2, 1, 256), -1, np.int32)
    for variant in range(2):
        z0 = -2 if variant == 0 else 0
        for d in range(n):
            for half in range(2):
                for xk in range(cx + 4):
                    for e in range(window):
                        x = (cx * d - 2 + xk) % total_x
                        z = z0 + e
                        t, zp = hops + z // zl, z % zl
                        src = half * nt * lanes + t * lanes + x * zl + zp
                        lane = half * 64 + xk * window + e
                        table[variant, d // 2, 0, (d % 2) * 128 + lane] = src
    return table


def spread_table(n, cx, zl, fine_z):
    window = zl + 2
    table = np.full((cx + 4, 1, 2 * fine_z), -1, np.int32)
    for k in range(cx + 4):
        for lane in range(2 * fine_z):
            if lane < fine_z + 4:
                z = lane // 2
            elif lane >= 2 * fine_z - 4:
                z = (lane - 2 * fine_z) // 2
            else:
                continue
            s = min(max(z // zl, 0), n - 1)
            z0 = -2 if s < n // 2 else 0
            table[k, 0, lane] = s * 64 + k * window + (z - s * zl - z0)
    return table


def step(velocity, w_in, w_mid_a, w_mid_b, w_out):
    n = lax.axis_size("slab")
    groups = lax.axis_size("grp")
    devices = n * groups
    comps, fine_x, fine_y, fine_z = velocity.shape
    cx, cy, cz = fine_x // 2, fine_y // 2, fine_z // 2
    zl = cz // n
    lanes = n * cx * zl
    hops = -(-MARGIN // zl)
    nt = 2 * hops + 1
    assert lanes == 128 and fine_z == 128 and cx == 2 and cy % 8 == 0 and (cx + 4) * (zl + 2) <= 64
    length = 6 * n * cx * cy * groups * cz
    both = ("grp", "slab")

    def ring(x, shift):
        return lax.ppermute(x, both, [(i, (i + shift) % devices) for i in range(devices)])

    def shift(x, axis, by):
        count = lax.axis_size(axis)
        return lax.ppermute(x, axis, [(i, (i + by) % count) for i in range(count)])

    spread = jnp.stack(
        [
            jnp.pad(w_in, ((0, 0), (0, 0), (0, CH - 3))),
            w_mid_a,
            w_mid_b,
            jnp.pad(w_out, ((0, 0), (3, CH - 9), (0, 0))),
        ]
    ).reshape(LAYERS, 3, 3, 3, CH, CH)
    w_fwd = jnp.transpose(spread, (0, 3, 4, 2, 1, 5)).reshape(LAYERS, 3 * CH, 9 * CH)
    w_bwd = jnp.transpose(spread[:, ::-1, ::-1, ::-1], (0, 3, 5, 2, 1, 4)).reshape(
        LAYERS, 3 * CH, 9 * CH
    )

    group = round_up(-(-9 * cy // n), 16)
    fields = call(
        functools.partial(filter_kernel, n),
        jax.ShapeDtypeStruct((n, group, lanes), bf16),
        [pltpu.VMEM((9 * cy, cx * fine_z), f32), pltpu.VMEM((n * group, lanes), f32)],
        4_000_000_000,
        1,
    )(velocity)
    mine = lax.all_to_all(fields, "slab", 0, 0, tiled=True)

    v16, edge = call(
        edge_kernel,
        (
            jax.ShapeDtypeStruct((comps * fine_x * fine_y, fine_z), bf16),
            jax.ShapeDtypeStruct((fine_y, 128), bf16),
        ),
        [],
        1_000_000_000,
        1,
    )(velocity)
    from_left = shift(edge, "grp", 1)
    from_right = shift(edge, "grp", -1)
    edges = jnp.concatenate([from_left, from_right], axis=0)

    lower = [ring(mine, k) for k in range(hops, 0, -1)]
    upper = [ring(mine, -k) for k in range(1, hops + 1)]
    edges, v16, lower, upper = lax.optimization_barrier((edges, v16, lower, upper))
    pack = jnp.concatenate([v16, edges], axis=0)
    pack_left = shift(pack, "slab", 1)
    pack_right = shift(pack, "slab", -1)

    place = lax.axis_index("slab")
    tables = send_table(n, hops, cx, zl, lanes)
    send_idx = jnp.where(place < n // 2, tables[0], tables[1])
    srows = round_up(-(-6 * (cy // groups) // n), 16)
    grad_rows = LAYERS * 3 * CH * 9 // 8
    per_device = round_up(-(-grad_rows // devices), 8)
    act = pltpu.VMEM((cy + 2, 3 * CH, nt * lanes), bf16)
    bsend, ssend, grads = call(
        functools.partial(
            closure_kernel, (n, hops, groups, devices, cy, cx, zl, length)
        ),
        (
            jax.ShapeDtypeStruct((n, 3 * cy, 128), bf16),
            jax.ShapeDtypeStruct((devices, srows, lanes), bf16),
            jax.ShapeDtypeStruct((devices * per_device, 128), f32),
        ),
        [
            act,
            act,
            act,
            act,
            act,
            pltpu.VMEM((cy, 3 * CH, lanes), bf16),
            pltpu.VMEM((nt, max(CH * cy, n * group), lanes), f32),
            pltpu.VMEM((n * srows, lanes), f32),
            pltpu.VMEM((LAYERS, 3 * CH, 9 * CH), f32),
        ],
        40_000_000_000,
        nt + 3,
    )(*lower, mine, *upper, w_fwd, w_bwd, send_idx)

    st = lax.all_to_all(bsend, "slab", 0, 0, tiled=True)
    partial_sums = lax.all_to_all(grads.reshape(devices, per_device, 128), both, 0, 0, tiled=True)
    total = jnp.sum(partial_sums, axis=0)
    summed = lax.all_to_all(
        jnp.broadcast_to(total[None], (devices, per_device, 128)), both, 0, 0, tiled=True
    ).reshape(devices * per_device, 128)
    out_blocks = lax.all_to_all(ssend, both, 0, 0, tiled=True)

    velocity_next = call(
        functools.partial(advance_kernel, n),
        jax.ShapeDtypeStruct(velocity.shape, f32),
        [
            pltpu.VMEM((comps, 3 * fine_x, fine_y + 16, 2 * fine_z), f32),
            pltpu.VMEM((comps, 2 * fine_x, fine_y + 16, 2 * fine_z), f32),
            pltpu.VMEM((6, cx + 4, cy + 16, 2 * fine_z), f32),
            pltpu.VMEM((2 * fine_z // 128, comps, 2 * fine_x, fine_y, 128), f32),
        ],
        15_000_000_000,
        6,
    )(velocity, edges, pack_left, pack_right, st, spread_table(n, cx, zl, fine_z))

    stress = call(
        functools.partial(stress_kernel, n, groups, zl),
        jax.ShapeDtypeStruct((6, cx, cy // groups, groups * cz), bf16),
        [pltpu.VMEM((groups, n * srows, lanes), f32)],
        1_000_000_000,
        1,
    )(out_blocks)
    grad_in, grad_mid_a, grad_mid_b, grad_out = call(
        unpack_kernel,
        (
            jax.ShapeDtypeStruct((27, CH, 3), f32),
            jax.ShapeDtypeStruct((27, CH, CH), f32),
            jax.ShapeDtypeStruct((27, CH, CH), f32),
            jax.ShapeDtypeStruct((27, 6, CH), f32),
        ),
        [],
        1_000_000_000,
        1,
    )(summed)
    return (velocity_next, stress, grad_in, grad_mid_a, grad_mid_b, grad_out)


def solution(mesh):
    in_specs = (P(None, "slab", None, "grp"), P(), P(), P(), P())
    out_specs = (P(None, "slab", None, "grp"), P(None, "slab", "grp", None), P(), P(), P(), P())
    return jax.shard_map(step, mesh=mesh, in_specs=in_specs, out_specs=out_specs, check_vma=False)
```

```python
import functools

import jax
import jax.numpy as jnp
import numpy as np
from jax import lax
from jax.experimental import pallas as pl
from jax.experimental.pallas import tpu as pltpu
from jax.sharding import PartitionSpec as P

step_size = 0.1
viscosity = 0.5
closure_weight = 4.0
pair_table = ((0, 3, 4), (3, 1, 5), (4, 5, 2))
stress_pairs = ((0, 0), (1, 1), (2, 2), (0, 1), (0, 2), (1, 2))
LAYERS = 4
CH = 16
SPAN = 3
MARGIN = LAYERS + LAYERS - 1
f32 = jnp.float32
bf16 = jnp.bfloat16
BATCH = 8
MIB = 1024 * 1024


def round_up(a, b):
    return -(-a // b) * b


def log2(n):
    assert n & (n - 1) == 0
    return n.bit_length() - 1


def nbytes(shapes):
    return sum(
        int(np.prod(x.shape)) * jnp.dtype(x.dtype).itemsize
        for x in shapes
        if hasattr(x, "memory_space") and x.memory_space == pltpu.VMEM
    )


def call(body, out_shape, scratch, cost, n_in, low=36, far_in=0, far_out=0):
    many = isinstance(out_shape, (tuple, list))
    grant = max(low * MIB, min(62 * MIB, int(1.1 * nbytes(scratch)) + 9 * MIB))
    spec = pl.BlockSpec(memory_space=pltpu.VMEM)
    far = pl.BlockSpec(memory_space=pltpu.HBM)
    return pl.pallas_call(
        body,
        out_shape=out_shape,
        in_specs=[spec] * (n_in - far_in) + [far] * far_in,
        out_specs=[spec] * (len(out_shape) - far_out) + [far] * far_out if many else spec,
        scratch_shapes=scratch,
        compiler_params=pltpu.CompilerParams(vmem_limit_bytes=grant),
        cost_estimate=pl.CostEstimate(flops=cost, bytes_accessed=cost // 400, transcendentals=0),
    )


def granule_swap(arrays):
    n = len(arrays)
    lanes = arrays[0].shape[1]
    gran = lanes // n
    granule = lax.broadcasted_iota(jnp.int32, arrays[0].shape, 1) >> log2(gran)
    arrays = list(arrays)
    hop = 1
    while hop < n:
        upper = (granule & hop) != 0
        for i in range(n):
            if i & hop:
                continue
            low, high = arrays[i], arrays[i + hop]
            arrays[i] = jnp.where(upper, pltpu.roll(high, hop * gran, 1), low)
            arrays[i + hop] = jnp.where(upper, high, pltpu.roll(low, lanes - hop * gran, 1))
        hop *= 2
    return arrays


def rounded(x):
    return x.astype(bf16).astype(f32)


def filter_kernel(n, v_ref, out_ref, q_ref, f_ref):
    _, fine_x, fine_y, fine_z = v_ref.shape
    cx, cy, cz = fine_x // 2, fine_y // 2, fine_z // 2
    zl = cz // n
    group = out_ref.shape[1]
    lanes = out_ref.shape[2]

    def chunk(j, carry):
        for xi in range(cx):
            sums = [None] * 9
            for a in range(2):
                for p in range(2):
                    cell = [v_ref[c, 2 * xi + a, pl.ds(16 * j + p, 8, stride=2), :] for c in range(3)]
                    terms = cell + [cell[l] * cell[r] for l, r in stress_pairs]
                    sums = [t if s is None else s + t for s, t in zip(sums, terms)]
            for k in range(9):
                q_ref[pl.ds(pl.multiple_of(k * cy + 8 * j, 8), 8), xi * fine_z : (xi + 1) * fine_z] = sums[k]
        return carry

    lax.fori_loop(0, cy // 8, chunk, 0)
    row = lax.broadcasted_iota(jnp.int32, (cx * fine_z, lanes), 0)
    col = lax.broadcasted_iota(jnp.int32, (cx * fine_z, lanes), 1)
    row_x = row >> log2(fine_z)
    row_z = (row & (fine_z - 1)) >> 1
    col_x = (col & (cx * zl - 1)) >> log2(zl)
    col_z = (col >> log2(cx * zl)) * zl + (col & (zl - 1))
    proj = jnp.where((row_x == col_x) & (row_z == col_z), 0.125, 0.0).astype(f32)
    means = []
    for k in range(9):
        mean = jnp.dot(
            q_ref[k * cy : (k + 1) * cy, :],
            proj,
            precision=lax.Precision.HIGHEST,
            preferred_element_type=f32,
        )
        if k < 3:
            means.append(mean)
        else:
            l, r = stress_pairs[k - 3]
            mean = mean - means[l] * means[r]
        f_ref[k * cy : (k + 1) * cy, :] = mean
    tail = n * group - 9 * cy
    if tail:
        f_ref[9 * cy :, :] = jnp.zeros((tail, lanes), f32)

    def swap(j, carry):
        base = pl.multiple_of(16 * j, 16)
        parts = granule_swap([f_ref[pl.ds(r * group + base, 16), :] for r in range(n)])
        for d in range(n):
            out_ref[d, pl.ds(base, 16), :] = parts[d].astype(bf16)
        return carry

    lax.fori_loop(0, group // 16, swap, 0)


def edge_kernel(v_ref, v16_ref, e_ref):
    comps, fine_x, fine_y, fine_z = v_ref.shape
    row = lax.broadcasted_iota(jnp.int32, (fine_z, 128), 0)
    col = lax.broadcasted_iota(jnp.int32, (fine_z, 128), 1)
    total = jnp.zeros((fine_y, 128), f32)
    for c in range(comps):
        for x in range(fine_x):
            block = v_ref[c, x].astype(bf16)
            base = (c * fine_x + x) * 8
            v16_ref[(c * fine_x + x) * fine_y : (c * fine_x + x + 1) * fine_y, :] = block
            e = col - base
            hit = ((e >= 0) & (e < 4) & (row == e)) | ((e >= 4) & (e < 8) & (row == fine_z - 8 + e))
            total = total + jnp.dot(
                block, jnp.where(hit, 1.0, 0.0).astype(bf16), preferred_element_type=f32
            )
    e_ref[...] = total.astype(bf16)


def closure_tools(nt, hops, lanes, zl, unroll):
    zpos = lax.broadcasted_iota(jnp.int32, (CH, lanes), 1) & (zl - 1)
    first_z = zpos == 0
    last_z = zpos == zl - 1

    def tile(value, t):
        t = min(max(t, 0), nt - 1)
        return value[:, t * lanes : (t + 1) * lanes]

    def after(value, t):
        return jnp.where(
            last_z, pltpu.roll(tile(value, t + 1), zl - 1, 1), pltpu.roll(tile(value, t), lanes - 1, 1)
        )

    def before(value, t):
        return jnp.where(
            first_z,
            pltpu.roll(tile(value, t - 1), lanes - (zl - 1), 1),
            pltpu.roll(tile(value, t), 1, 1),
        )

    def put(ref, y, value):
        for t in range(nt):
            v = tile(value, t)
            at = slice(t * lanes, (t + 1) * lanes)
            ref[y + 1, 0:CH, at] = pltpu.roll(v, zl, 1).astype(bf16)
            ref[y + 1, CH : 2 * CH, at] = v.astype(bf16)
            ref[y + 1, 2 * CH : 3 * CH, at] = pltpu.roll(v, lanes - zl, 1).astype(bf16)

    def put_cz(cz_ref, y, value):
        value = rounded(value)
        cz_ref[y, 0:CH, :] = after(value, hops).astype(bf16)
        cz_ref[y, CH : 2 * CH, :] = tile(value, hops).astype(bf16)
        cz_ref[y, 2 * CH : 3 * CH, :] = before(value, hops).astype(bf16)

    def convolve(src, w, ys):
        sums = []
        for first in range(0, len(ys), 2 * SPAN):
            columns = jnp.concatenate(
                [
                    src[pl.ds(ys[at], SPAN + 2)].reshape((SPAN + 2) * 3 * CH, nt * lanes)
                    for at in range(first, first + 2 * SPAN, SPAN)
                ],
                axis=1,
            )
            results = jnp.dot(w, columns, preferred_element_type=f32)
            for u in range(2 * SPAN):
                at = (u // SPAN) * nt * lanes
                parts = results[
                    (u % SPAN) * 3 * CH : (u % SPAN + 1) * 3 * CH, at : at + nt * lanes
                ]
                low, mid, high = parts[0:CH], parts[CH : 2 * CH], parts[2 * CH :]
                sums.append(
                    jnp.concatenate(
                        [tile(mid, t) + before(low, t) + after(high, t) for t in range(nt)], axis=1
                    )
                )
        return sums

    def rows_at(j):
        return [unroll * j + u for u in range(unroll)]

    return tile, put, put_cz, convolve, rows_at


def stored(far_ref, i, near_ref):
    rows, _, columns = near_ref.shape
    return far_ref.at[i, 0:rows, :, 0:columns]


def forward_kernel(dims, *refs):
    n, hops, groups, _, cy, _, zl, length, unroll = dims
    nt = 2 * hops + 1
    tiles = refs[:nt]
    wf_ref, idx_ref = refs[nt : nt + 2]
    bsend_ref, ssend_ref = refs[nt + 2 : nt + 4]
    far_ref = refs[nt + 4]
    acts = refs[nt + 5 : nt + 9]
    cot_ref, cz_ref, f_ref, fs_ref, sems = refs[nt + 9 :]
    near = (*acts, cot_ref, cz_ref)

    def save(i):
        return pltpu.make_async_copy(near[i], stored(far_ref, i, near[i]), sems.at[i])

    group = tiles[0].shape[1]
    lanes = tiles[0].shape[2]
    tile, put, put_cz, convolve, rows_at = closure_tools(nt, hops, lanes, zl, unroll)

    for ref in (*acts, cot_ref):
        zero = jnp.zeros((3 * CH, nt * lanes), bf16)
        ref[0] = zero
        ref[cy + 1] = zero
    for t in range(nt):
        used = n * group
        if used < CH * cy:
            f_ref[t, used:, :] = jnp.zeros((CH * cy - used, lanes), f32)

        def swap(j, carry, t=t):
            base = pl.multiple_of(16 * j, 16)
            parts = granule_swap([tiles[t][s, pl.ds(base, 16), :].astype(f32) for s in range(n)])
            for r in range(n):
                f_ref[t, pl.ds(r * group + base, 16), :] = parts[r]
            return carry

        lax.fori_loop(0, group // 16, swap, 0)

    def load_fields(y):
        return jnp.concatenate([f_ref[t, pl.ds(y, CH, stride=cy), :] for t in range(nt)], axis=1)

    def start(j, carry):
        for y in rows_at(j):
            put(acts[0], y, load_fields(y))
        return carry

    lax.fori_loop(0, cy // unroll, start, 0)
    save(0).start()

    for k in range(LAYERS - 1):
        w = wf_ref[k]

        def forward(j, carry, k=k, w=w):
            ys = rows_at(j)
            outs = [jnp.tanh(v) for v in convolve(acts[k], w, ys)]
            for y, v in zip(ys, outs):
                put(acts[k + 1], y, v)
            return carry

        lax.fori_loop(0, cy // unroll, forward, 0)
        save(k + 1).start()

    w_last = wf_ref[LAYERS - 1]
    channel = lax.broadcasted_iota(jnp.int32, (CH, nt * lanes), 0)
    stressed = (channel >= 3) & (channel < 9)

    def predict(j, carry):
        ys = rows_at(j)
        targets = [load_fields(y) for y in ys]
        predicted = convolve(acts[LAYERS - 1], w_last, ys)
        cots = [
            jnp.where(stressed, 2.0 / length * (v - target), 0.0)
            for v, target in zip(predicted, targets)
        ]
        for y, cot in zip(ys, cots):
            put(cot_ref, y, cot)
            put_cz(cz_ref, y, cot)
        for y, v in zip(ys, predicted):
            stress = rounded(v)
            for t in range(nt):
                f_ref[t, pl.ds(y, CH, stride=cy), :] = tile(stress, t)
        return carry

    lax.fori_loop(0, cy // unroll, predict, 0)
    save(LAYERS).start()
    save(LAYERS + 1).start()

    left = jnp.concatenate(
        [
            f_ref[t, (3 + 3 * half) * cy : (6 + 3 * half) * cy, :].astype(bf16)
            for half in range(2)
            for t in range(nt)
        ],
        axis=1,
    )
    row = lax.broadcasted_iota(jnp.int32, (2 * nt * lanes, 256), 0)
    for d in range(n // 2):
        pick = jnp.where(row == idx_ref[d], 1.0, 0.0).astype(bf16)
        moved = jnp.dot(left, pick, preferred_element_type=f32).astype(bf16)
        bsend_ref[2 * d] = moved[:, 0:128]
        bsend_ref[2 * d + 1] = moved[:, 128:256]

    wide = cy // groups
    srows = ssend_ref.shape[1]
    fs_ref[...] = jnp.zeros(fs_ref.shape, f32)
    for g in range(groups):
        for c in range(6):
            at = (3 + c) * cy + g * wide
            fs_ref[c * wide : (c + 1) * wide, :] = f_ref[hops, at : at + wide, :]
        for j in range(srows // 16):
            parts = granule_swap(
                [fs_ref[r * srows + 16 * j : r * srows + 16 * j + 16, :] for r in range(n)]
            )
            for d in range(n):
                ssend_ref[g * n + d, 16 * j : 16 * j + 16, :] = parts[d]
    for i in range(LAYERS + 2):
        save(i).wait()


def backward_kernel(dims, *refs):
    _, hops, _, devices, cy, _, zl, _, unroll = dims
    nt = 2 * hops + 1
    wb_ref, ssend_ref = refs[:2]
    far_ref, sum_ref = refs[2:4]
    acts = refs[4:8]
    cot_ref, cz_in_ref, cz_ref, g_ref, grad_ref, sems = refs[8:]
    near = (*acts, cot_ref, cz_in_ref)

    def fetch(i):
        return pltpu.make_async_copy(stored(far_ref, i, near[i]), near[i], sems.at[i])

    for i in (LAYERS + 1, LAYERS - 1, LAYERS, *range(LAYERS - 2, -1, -1)):
        fetch(i).start()
    lanes = ssend_ref.shape[2]
    own = hops * lanes
    _, put, put_cz, convolve, rows_at = closure_tools(nt, hops, lanes, zl, unroll)

    def weight_gradient(src, cz_ref, k):
        def pair(j, acc):
            ys = [BATCH * j + u for u in range(BATCH)]
            left = jnp.concatenate([cz_ref[y] for y in ys], axis=1)
            right = jnp.concatenate(
                [src[pl.ds(y, 3), :, own : own + lanes].reshape(9 * CH, lanes) for y in ys],
                axis=1,
            )
            return acc + lax.dot_general(
                left, right, (((1,), (1,)), ((), ())), preferred_element_type=f32
            )

        g_ref[k] = lax.fori_loop(0, cy // BATCH, pair, jnp.zeros((3 * CH, 9 * CH), f32))

    fetch(LAYERS + 1).wait()
    fetch(LAYERS - 1).wait()
    weight_gradient(acts[LAYERS - 1], cz_in_ref, LAYERS - 1)
    fetch(LAYERS).wait()
    source = cot_ref
    for k in range(LAYERS - 1, 0, -1):
        w = wb_ref[k]
        here = acts[k]

        def backward(j, carry, w=w, here=here, source=source, k=k):
            ys = rows_at(j)
            below = [here[y + 1, CH : 2 * CH, :].astype(f32) for y in ys]
            cots = [v * (1.0 - b * b) for v, b in zip(convolve(source, w, ys), below)]
            for y, cot in zip(ys, cots):
                if k > 1:
                    put(here, y, cot)
                put_cz(cz_ref, y, cot)
            return carry

        lax.fori_loop(0, cy // unroll, backward, 0)
        fetch(k - 1).wait()
        weight_gradient(acts[k - 1], cz_ref, k - 1)
        source = here

    rows = LAYERS * 3 * CH
    main = 8 * CH
    rest = jnp.zeros((rows // 8, main), f32)
    for k in range(LAYERS):
        grad_ref[k * 3 * CH : (k + 1) * 3 * CH, :] = g_ref[k, :, 0:main]
        for half in range(2):
            j = 2 * k + half
            piece = g_ref[k, half * 24 : half * 24 + 24, main:]
            piece = jnp.concatenate([piece, jnp.zeros((24, main - CH), f32)], axis=1)
            rest = rest + (pltpu.roll(piece, j * CH, 1) if j else piece)
    grad_ref[rows : rows + rows // 8, :] = rest
    if grad_ref.shape[0] > rows + rows // 8:
        grad_ref[rows + rows // 8 :, :] = jnp.zeros(
            (grad_ref.shape[0] - rows - rows // 8, main), f32
        )

    share = grad_ref.shape[0] // devices
    for d in range(devices):
        sum_ref[d, 0:share, :] = grad_ref[d * share : (d + 1) * share, :]
        sum_ref[d, share:, :] = ssend_ref[d]


def stress_kernel(n, groups, zl, recv_ref, out_ref, fs_ref):
    comps, cx, wide, _ = out_ref.shape
    srows = fs_ref.shape[1] // n
    skip = recv_ref.shape[1] - srows
    lanes = recv_ref.shape[2]
    cz = n * zl
    for g in range(groups):
        for j in range(srows // 16):
            parts = granule_swap(
                [
                    recv_ref[g * n + s, skip + 16 * j : skip + 16 * j + 16, :]
                    for s in range(n)
                ]
            )
            for r in range(n):
                fs_ref[g, r * srows + 16 * j : r * srows + 16 * j + 16, :] = parts[r]
    row = lax.broadcasted_iota(jnp.int32, (2 * lanes, 2 * cz), 0)
    col = lax.broadcasted_iota(jnp.int32, (2 * lanes, 2 * cz), 1)
    z = col & (cz - 1)
    need = (col >> log2(cz)) * lanes + (z >> log2(zl)) * (cx * zl) + (z & (zl - 1))
    used = round_up(comps * wide, 8)
    for xi in range(cx):
        pick = jnp.where(row == need + xi * zl, 1.0, 0.0).astype(bf16)
        for pair in range(groups // 2):
            left = jnp.concatenate(
                [fs_ref[2 * pair, 0:used, :], fs_ref[2 * pair + 1, 0:used, :]], axis=1
            ).astype(bf16)
            moved = jnp.dot(left, pick, preferred_element_type=f32)
            for c in range(comps):
                out_ref[c, xi, :, 2 * cz * pair : 2 * cz * (pair + 1)] = moved[
                    c * wide : (c + 1) * wide
                ].astype(bf16)


def unpack_kernel(all_ref, in_ref, mid_a_ref, mid_b_ref, out_ref):
    rows = LAYERS * 3 * CH
    main = 8 * CH
    rest = all_ref[rows : rows + rows // 8, :]
    for k, (ref, first, count, inputs) in enumerate(
        ((in_ref, 0, CH, 3), (mid_a_ref, 0, CH, CH), (mid_b_ref, 0, CH, CH), (out_ref, 3, 6, CH))
    ):
        block = all_ref[k * 3 * CH : (k + 1) * 3 * CH, :]
        tails = []
        for half in range(2):
            j = 2 * k + half
            tails.append(pltpu.roll(rest, main - j * CH, 1) if j else rest)
        tail = jnp.concatenate(tails, axis=0)
        for dy in range(3):
            for dx in range(3):
                at = dy * 3 + dx
                if at == 8:
                    moved = tail
                else:
                    moved = pltpu.roll(block, main - at * CH, 1) if at else block
                for dz in range(3):
                    ref[(dx * 3 + dy) * 3 + dz] = moved[
                        dz * CH + first : dz * CH + first + count, 0:inputs
                    ]


def tendency(ref, x, y0, rows, forcing):
    wide = ref.shape[-1]

    def at(c, dx, dy):
        return ref[c, x + dx, y0 + 8 + dy : y0 + 8 + dy + rows, :]

    centre = [at(c, 0, 0) for c in range(3)]
    results = []
    for i in range(3):
        f0 = centre[i]
        total = None
        for j in range(3):
            if j == 0:
                m2, m1, p1, p2 = (at(i, k, 0) for k in (-2, -1, 1, 2))
            elif j == 1:
                m2, m1, p1, p2 = (at(i, 0, k) for k in (-2, -1, 1, 2))
            else:
                m2, m1, p1, p2 = (pltpu.roll(f0, (-k) % wide, 1) for k in (-2, -1, 1, 2))
            slope = 8.0 * (p1 - m1) - (p2 - m2)
            curve = 16.0 * (p1 + m1) - (p2 + m2) - 30.0 * f0
            term = viscosity * curve - centre[j] * slope
            total = term if total is None else total + term
        results.append((f0, total / 12.0 + forcing[i]))
    return results


def advance_kernel(n, v_ref, ez_ref, xl_ref, xr_ref, st_ref, idx_ref, out_ref, u_ref, f1_ref, t_ref, frc_ref):
    comps, fine_x, fine_y, fine_z = v_ref.shape
    cy = fine_y // 2
    wide = 2 * fine_z
    pad = jnp.zeros((8, wide), f32)
    rows_v = comps * fine_x * fine_y
    for c in range(comps):
        for x in range(3 * fine_x):
            u_ref[c, x, 0:8, :] = pad
            u_ref[c, x, fine_y + 8 : fine_y + 16, :] = pad
        for x in range(fine_x):
            at = slice((c * fine_x + x) * fine_y, (c * fine_x + x + 1) * fine_y)
            u_ref[c, x, 8 : fine_y + 8, 0:fine_z] = xl_ref[at, :].astype(f32)
            u_ref[c, fine_x + x, 8 : fine_y + 8, 0:fine_z] = v_ref[c, x]
            u_ref[c, 2 * fine_x + x, 8 : fine_y + 8, 0:fine_z] = xr_ref[at, :].astype(f32)
        for x in range(2 * fine_x):
            f1_ref[c, x, 0:8, :] = pad
            f1_ref[c, x, fine_y + 8 : fine_y + 16, :] = pad
    edges = jnp.concatenate(
        [
            jnp.concatenate([ref[at : at + fine_y, :], ref[at + fine_y : at + 2 * fine_y, :]], axis=1)
            for ref, at in ((xl_ref, rows_v), (ez_ref, 0), (xr_ref, rows_v))
        ],
        axis=0,
    )
    row = lax.broadcasted_iota(jnp.int32, (256, 2 * fine_z), 0)
    col = lax.broadcasted_iota(jnp.int32, (256, 2 * fine_z), 1)
    lane = col & (fine_z - 1)
    for c in range(comps):
        for x in range(0, fine_x, 2):
            base = (c * fine_x + x) * 8 + (col >> log2(fine_z)) * 8
            need = jnp.where(lane < 4, 128 + base + lane, base + lane - (fine_z - 8))
            hit = (row == need) & ((lane < 4) | (lane >= fine_z - 4))
            moved = jnp.dot(
                edges, jnp.where(hit, 1.0, 0.0).astype(bf16), preferred_element_type=f32
            )
            for s in range(3):
                for e in range(2):
                    u_ref[c, s * fine_x + x + e, 8 : fine_y + 8, fine_z:wide] = moved[
                        s * fine_y : (s + 1) * fine_y, e * fine_z : (e + 1) * fine_z
                    ]

    half_lane = lax.broadcasted_iota(jnp.int32, (3 * cy, 128), 1) < 64
    lows, highs = [], []
    for s in range(0, n, 2):
        a, b = st_ref[s].astype(f32), st_ref[s + 1].astype(f32)
        lows.append(jnp.where(half_lane, a, pltpu.roll(b, 64, 1)).astype(bf16))
        highs.append(jnp.where(half_lane, pltpu.roll(a, 64, 1), b).astype(bf16))
    low = jnp.concatenate(lows, axis=1)
    high = jnp.concatenate(highs, axis=1)
    row = lax.broadcasted_iota(jnp.int32, (64 * n, wide), 0)
    for k in range(6):
        pick = jnp.where(row == idx_ref[k], 1.0, 0.0).astype(bf16)
        for h, src in enumerate((low, high)):
            moved = jnp.dot(src, pick, preferred_element_type=f32)
            for c in range(3):
                t_ref[3 * h + c, k, 0:8, :] = pad
                t_ref[3 * h + c, k, cy + 8 : cy + 16, :] = pad
                t_ref[3 * h + c, k, 8 : cy + 8, :] = moved[c * cy : (c + 1) * cy]

    scale = -closure_weight / 12.0

    def force(kk, carry):
        k = kk + 1
        for y0 in range(0, cy, 8):
            for i in range(3):
                ax, ay, az = pair_table[i]
                tz = t_ref[az, k, y0 + 8 : y0 + 16, :]
                m2, m1, p1, p2 = (pltpu.roll(tz, (-e) % wide, 1) for e in (-2, -1, 1, 2))
                along_z = 8.0 * (p1 - m1) - (p2 - m2)
                m, o, p = (t_ref[ay, k, y0 + 8 + e : y0 + 16 + e, :] for e in (-1, 0, 1))
                even = along_z + (8.0 * o - 7.0 * m - p)
                odd = along_z + (7.0 * p - 8.0 * o + m)
                m, o, p = (t_ref[ax, k + e, y0 + 8 : y0 + 16, :] for e in (-1, 0, 1))
                for px in range(2):
                    along_x = 7.0 * p - 8.0 * o + m if px else 8.0 * o - 7.0 * m - p
                    for py, part in enumerate((even, odd)):
                        value = scale * (along_x + part)
                        for h in range(0, wide, 128):
                            frc_ref[
                                h // 128, i, 2 * kk + px, pl.ds(2 * y0 + py, 8, stride=2), :
                            ] = value[:, h : h + 128]
        return carry

    lax.fori_loop(0, fine_x, force, 0)

    def forcing_at(x, y0):
        return [
            jnp.concatenate(
                [frc_ref[h, i, x, y0 : y0 + rows, :] for h in range(wide // 128)], axis=1
            )
            for i in range(3)
        ]

    rows = 8

    def one(x, carry):
        for y0 in range(0, fine_y, rows):
            for i, (f0, t) in enumerate(tendency(u_ref, x + 2, y0, rows, forcing_at(x, y0))):
                f1_ref[i, x, y0 + 8 : y0 + 8 + rows, :] = f0 + step_size * t
        return carry

    lax.fori_loop(0, 2 * fine_x, one, 0)

    def two(x, carry):
        for y0 in range(0, fine_y, rows):
            for i, (f0, t) in enumerate(tendency(f1_ref, x + 2, y0, rows, forcing_at(x + 2, y0))):
                nxt = (f0 + step_size * t)[:, 0:fine_z]
                out_ref[i, x, y0 : y0 + rows, :] = 0.5 * (v_ref[i, x, y0 : y0 + rows, :] + nxt)
        return carry

    lax.fori_loop(0, fine_x, two, 0)


def send_table(n, hops, cx, zl, lanes):
    nt = 2 * hops + 1
    total_x = n * cx
    window = zl + 2
    table = np.full((2, n // 2, 1, 256), -1, np.int32)
    for variant in range(2):
        z0 = -2 if variant == 0 else 0
        for d in range(n):
            for half in range(2):
                for xk in range(cx + 4):
                    for e in range(window):
                        x = (cx * d - 2 + xk) % total_x
                        z = z0 + e
                        t, zp = hops + z // zl, z % zl
                        src = half * nt * lanes + t * lanes + x * zl + zp
                        lane = half * 64 + xk * window + e
                        table[variant, d // 2, 0, (d % 2) * 128 + lane] = src
    return table


def spread_table(n, cx, zl, fine_z):
    window = zl + 2
    table = np.full((cx + 4, 1, 2 * fine_z), -1, np.int32)
    for k in range(cx + 4):
        for lane in range(2 * fine_z):
            if lane < fine_z + 4:
                z = lane // 2
            elif lane >= 2 * fine_z - 4:
                z = (lane - 2 * fine_z) // 2
            else:
                continue
            s = min(max(z // zl, 0), n - 1)
            z0 = -2 if s < n // 2 else 0
            table[k, 0, lane] = s * 64 + k * window + (z - s * zl - z0)
    return table


def step(velocity, w_in, w_mid_a, w_mid_b, w_out):
    n = lax.axis_size("slab")
    groups = lax.axis_size("grp")
    devices = n * groups
    comps, fine_x, fine_y, fine_z = velocity.shape
    cx, cy, cz = fine_x // 2, fine_y // 2, fine_z // 2
    zl = cz // n
    lanes = n * cx * zl
    hops = -(-MARGIN // zl)
    nt = 2 * hops + 1
    assert lanes == 128 and fine_z == 128 and cx == 2 and cy % 8 == 0 and (cx + 4) * (zl + 2) <= 64
    length = 6 * n * cx * cy * groups * cz
    both = ("grp", "slab")

    def ring(x, shift):
        return lax.ppermute(x, both, [(i, (i + shift) % devices) for i in range(devices)])

    def shift(x, axis, by):
        count = lax.axis_size(axis)
        return lax.ppermute(x, axis, [(i, (i + by) % count) for i in range(count)])

    spread = jnp.stack(
        [
            jnp.pad(w_in, ((0, 0), (0, 0), (0, CH - 3))),
            w_mid_a,
            w_mid_b,
            jnp.pad(w_out, ((0, 0), (3, CH - 9), (0, 0))),
        ]
    ).reshape(LAYERS, 3, 3, 3, CH, CH)
    w_fwd = jnp.transpose(spread, (0, 3, 4, 2, 1, 5)).reshape(LAYERS, 3 * CH, 9 * CH)
    w_bwd = jnp.transpose(spread[:, ::-1, ::-1, ::-1], (0, 3, 5, 2, 1, 4)).reshape(
        LAYERS, 3 * CH, 9 * CH
    )

    w_fwd, w_bwd = (
        jnp.concatenate(
            [
                jnp.pad(w, ((0, 0), (0, 0), (3 * CH * u, 3 * CH * (SPAN - 1 - u))))
                for u in range(SPAN)
            ],
            axis=1,
        )
        for w in (w_fwd, w_bwd)
    )

    group = round_up(-(-9 * cy // n), 16)
    fields = call(
        functools.partial(filter_kernel, n),
        jax.ShapeDtypeStruct((n, group, lanes), bf16),
        [pltpu.VMEM((9 * cy, cx * fine_z), f32), pltpu.VMEM((n * group, lanes), f32)],
        4_000_000_000,
        1,
    )(velocity)
    mine = lax.all_to_all(fields, "slab", 0, 0, tiled=True)

    v16, edge = call(
        edge_kernel,
        (
            jax.ShapeDtypeStruct((comps * fine_x * fine_y, fine_z), bf16),
            jax.ShapeDtypeStruct((fine_y, 128), bf16),
        ),
        [],
        1_000_000_000,
        1,
    )(velocity)
    from_left = shift(edge, "grp", 1)
    from_right = shift(edge, "grp", -1)
    edges = jnp.concatenate([from_left, from_right], axis=0)

    lower = [ring(mine, k) for k in range(hops, 0, -1)]
    upper = [ring(mine, -k) for k in range(1, hops + 1)]
    edges, v16, lower, upper = lax.optimization_barrier((edges, v16, lower, upper))
    pack = jnp.concatenate([v16, edges], axis=0)
    pack_left = shift(pack, "slab", 1)
    pack_right = shift(pack, "slab", -1)

    place = lax.axis_index("slab")
    tables = send_table(n, hops, cx, zl, lanes)
    send_idx = jnp.where(place < n // 2, tables[0], tables[1])
    srows = round_up(-(-6 * (cy // groups) // n), 16)
    grad_rows = LAYERS * 3 * CH * 9 // 8
    per_device = round_up(-(-grad_rows // devices), 8)
    act = pltpu.VMEM((cy + 2, 3 * CH, nt * lanes), bf16)
    unroll = max(
        u for u in range(1, cy + 1) if cy % u == 0 and u % (2 * SPAN) == 0 and u * nt <= 54
    )
    dims = (n, hops, groups, devices, cy, cx, zl, length, unroll)
    act = ((cy + 2, 3 * CH, nt * lanes), bf16)
    cz_shape = ((cy, 3 * CH, lanes), bf16)
    bsend, ssend, saved = call(
        functools.partial(forward_kernel, dims),
        (
            jax.ShapeDtypeStruct((n, 3 * cy, 128), bf16),
            jax.ShapeDtypeStruct((devices, srows, lanes), f32),
            jax.ShapeDtypeStruct((LAYERS + 2, *act[0]), bf16),
        ),
        [
            *[pltpu.VMEM(*act)] * (LAYERS + 1),
            pltpu.VMEM(*cz_shape),
            pltpu.VMEM((nt, max(CH * cy, n * group), lanes), f32),
            pltpu.VMEM((n * srows, lanes), f32),
            pltpu.SemaphoreType.DMA((LAYERS + 2,)),
        ],
        20_000_000_000,
        nt + 2,
        low=52,
        far_out=1,
    )(*lower, mine, *upper, w_fwd, send_idx)
    to_sum = call(
        functools.partial(backward_kernel, dims),
        jax.ShapeDtypeStruct((devices, per_device + srows, lanes), f32),
        [
            *[pltpu.VMEM(*act)] * (LAYERS + 1),
            pltpu.VMEM(*cz_shape),
            pltpu.VMEM(*cz_shape),
            pltpu.VMEM((LAYERS, 3 * CH, 9 * CH), f32),
            pltpu.VMEM((devices * per_device, lanes), f32),
            pltpu.SemaphoreType.DMA((LAYERS + 2,)),
        ],
        20_000_000_000,
        3,
        low=52,
        far_in=1,
    )(w_bwd, ssend, saved)

    st = lax.all_to_all(bsend, "slab", 0, 0, tiled=True)
    arrived = lax.all_to_all(to_sum, both, 0, 0, tiled=True)
    total = jnp.sum(arrived[:, :per_device], axis=0)
    summed = lax.all_to_all(
        jnp.broadcast_to(total[None], (devices, per_device, 128)), both, 0, 0, tiled=True
    ).reshape(devices * per_device, 128)
    velocity_next = call(
        functools.partial(advance_kernel, n),
        jax.ShapeDtypeStruct(velocity.shape, f32),
        [
            pltpu.VMEM((comps, 3 * fine_x, fine_y + 16, 2 * fine_z), f32),
            pltpu.VMEM((comps, 2 * fine_x, fine_y + 16, 2 * fine_z), f32),
            pltpu.VMEM((6, cx + 4, cy + 16, 2 * fine_z), f32),
            pltpu.VMEM((2 * fine_z // 128, comps, 2 * fine_x, fine_y, 128), f32),
        ],
        15_000_000_000,
        6,
    )(velocity, edges, pack_left, pack_right, st, spread_table(n, cx, zl, fine_z))

    stress = call(
        functools.partial(stress_kernel, n, groups, zl),
        jax.ShapeDtypeStruct((6, cx, cy // groups, groups * cz), bf16),
        [pltpu.VMEM((groups, n * srows, lanes), f32)],
        1_000_000_000,
        1,
    )(arrived)
    grad_in, grad_mid_a, grad_mid_b, grad_out = call(
        unpack_kernel,
        (
            jax.ShapeDtypeStruct((27, CH, 3), f32),
            jax.ShapeDtypeStruct((27, CH, CH), f32),
            jax.ShapeDtypeStruct((27, CH, CH), f32),
            jax.ShapeDtypeStruct((27, 6, CH), f32),
        ),
        [],
        1_000_000_000,
        1,
    )(summed)
    return (velocity_next, stress, grad_in, grad_mid_a, grad_mid_b, grad_out)


def solution(mesh):
    in_specs = (P(None, "slab", None, "grp"), P(), P(), P(), P())
    out_specs = (P(None, "slab", None, "grp"), P(None, "slab", "grp", None), P(), P(), P(), P())
    return jax.shard_map(step, mesh=mesh, in_specs=in_specs, out_specs=out_specs, check_vma=False)
```

```python
import functools

import jax
import jax.numpy as jnp
import numpy as np
from jax import lax
from jax.experimental import pallas as pl
from jax.experimental.pallas import tpu as pltpu
from jax.sharding import PartitionSpec as P

step_size = 0.1
viscosity = 0.5
closure_weight = 4.0
pair_table = ((0, 3, 4), (3, 1, 5), (4, 5, 2))
stress_pairs = ((0, 0), (1, 1), (2, 2), (0, 1), (0, 2), (1, 2))
LAYERS = 4
CH = 16
SPAN = 3
MARGIN = LAYERS + LAYERS - 1
f32 = jnp.float32
bf16 = jnp.bfloat16
BATCH = 24
MIB = 1024 * 1024


def round_up(a, b):
    return -(-a // b) * b


def log2(n):
    assert n & (n - 1) == 0
    return n.bit_length() - 1


def nbytes(shapes):
    return sum(
        int(np.prod(x.shape)) * jnp.dtype(x.dtype).itemsize
        for x in shapes
        if hasattr(x, "memory_space") and x.memory_space == pltpu.VMEM
    )


def call(body, out_shape, scratch, cost, n_in, low=36, far_in=0, far_out=0):
    many = isinstance(out_shape, (tuple, list))
    grant = max(low * MIB, min(62 * MIB, int(1.1 * nbytes(scratch)) + 9 * MIB))
    spec = pl.BlockSpec(memory_space=pltpu.VMEM)
    far = pl.BlockSpec(memory_space=pltpu.HBM)
    return pl.pallas_call(
        body,
        out_shape=out_shape,
        in_specs=[spec] * (n_in - far_in) + [far] * far_in,
        out_specs=[spec] * (len(out_shape) - far_out) + [far] * far_out if many else spec,
        scratch_shapes=scratch,
        compiler_params=pltpu.CompilerParams(vmem_limit_bytes=grant),
        cost_estimate=pl.CostEstimate(flops=cost, bytes_accessed=cost // 400, transcendentals=0),
    )


def granule_swap(arrays):
    n = len(arrays)
    lanes = arrays[0].shape[1]
    gran = lanes // n
    granule = lax.broadcasted_iota(jnp.int32, arrays[0].shape, 1) >> log2(gran)
    arrays = list(arrays)
    hop = 1
    while hop < n:
        upper = (granule & hop) != 0
        for i in range(n):
            if i & hop:
                continue
            low, high = arrays[i], arrays[i + hop]
            arrays[i] = jnp.where(upper, pltpu.roll(high, hop * gran, 1), low)
            arrays[i + hop] = jnp.where(upper, high, pltpu.roll(low, lanes - hop * gran, 1))
        hop *= 2
    return arrays


def rounded(x):
    return x.astype(bf16).astype(f32)


def filter_kernel(n, v_ref, out_ref, q_ref, f_ref):
    _, fine_x, fine_y, fine_z = v_ref.shape
    cx, cy, cz = fine_x // 2, fine_y // 2, fine_z // 2
    zl = cz // n
    group = out_ref.shape[1]
    lanes = out_ref.shape[2]

    def chunk(j, carry):
        for xi in range(cx):
            sums = [None] * 9
            for a in range(2):
                for p in range(2):
                    cell = [v_ref[c, 2 * xi + a, pl.ds(16 * j + p, 8, stride=2), :] for c in range(3)]
                    terms = cell + [cell[l] * cell[r] for l, r in stress_pairs]
                    sums = [t if s is None else s + t for s, t in zip(sums, terms)]
            for k in range(9):
                q_ref[pl.ds(pl.multiple_of(k * cy + 8 * j, 8), 8), xi * fine_z : (xi + 1) * fine_z] = sums[k]
        return carry

    lax.fori_loop(0, cy // 8, chunk, 0)
    row = lax.broadcasted_iota(jnp.int32, (cx * fine_z, lanes), 0)
    col = lax.broadcasted_iota(jnp.int32, (cx * fine_z, lanes), 1)
    row_x = row >> log2(fine_z)
    row_z = (row & (fine_z - 1)) >> 1
    col_x = (col & (cx * zl - 1)) >> log2(zl)
    col_z = (col >> log2(cx * zl)) * zl + (col & (zl - 1))
    proj = jnp.where((row_x == col_x) & (row_z == col_z), 0.125, 0.0).astype(f32)
    means = []
    for k in range(9):
        mean = jnp.dot(
            q_ref[k * cy : (k + 1) * cy, :],
            proj,
            precision=lax.Precision.HIGHEST,
            preferred_element_type=f32,
        )
        if k < 3:
            means.append(mean)
        else:
            l, r = stress_pairs[k - 3]
            mean = mean - means[l] * means[r]
        f_ref[k * cy : (k + 1) * cy, :] = mean
    tail = n * group - 9 * cy
    if tail:
        f_ref[9 * cy :, :] = jnp.zeros((tail, lanes), f32)

    def swap(j, carry):
        base = pl.multiple_of(16 * j, 16)
        parts = granule_swap([f_ref[pl.ds(r * group + base, 16), :] for r in range(n)])
        for d in range(n):
            out_ref[d, pl.ds(base, 16), :] = parts[d].astype(bf16)
        return carry

    lax.fori_loop(0, group // 16, swap, 0)


def edge_kernel(v_ref, v16_ref, e_ref):
    comps, fine_x, fine_y, fine_z = v_ref.shape
    row = lax.broadcasted_iota(jnp.int32, (fine_z, 128), 0)
    col = lax.broadcasted_iota(jnp.int32, (fine_z, 128), 1)
    total = jnp.zeros((fine_y, 128), f32)
    for c in range(comps):
        for x in range(fine_x):
            block = v_ref[c, x].astype(bf16)
            base = (c * fine_x + x) * 8
            v16_ref[(c * fine_x + x) * fine_y : (c * fine_x + x + 1) * fine_y, :] = block
            e = col - base
            hit = ((e >= 0) & (e < 4) & (row == e)) | ((e >= 4) & (e < 8) & (row == fine_z - 8 + e))
            total = total + jnp.dot(
                block, jnp.where(hit, 1.0, 0.0).astype(bf16), preferred_element_type=f32
            )
    e_ref[...] = total.astype(bf16)


def closure_tools(nt, hops, lanes, zl, unroll):
    zpos = lax.broadcasted_iota(jnp.int32, (CH, lanes), 1) & (zl - 1)
    first_z = zpos == 0
    last_z = zpos == zl - 1

    def tile(value, t):
        t = min(max(t, 0), nt - 1)
        return value[:, t * lanes : (t + 1) * lanes]

    def after(value, t):
        mixed = jnp.where(first_z, tile(value, t + 1), tile(value, t))
        return pltpu.roll(mixed, lanes - 1, 1)

    def before(value, t):
        mixed = jnp.where(last_z, tile(value, t - 1), tile(value, t))
        return pltpu.roll(mixed, 1, 1)

    def put(ref, y, value):
        for t in range(nt):
            v = tile(value, t).astype(bf16)
            at = slice(t * lanes, (t + 1) * lanes)
            ref[y + 1, 0:CH, at] = pltpu.roll(v, zl, 1)
            ref[y + 1, CH : 2 * CH, at] = v
            ref[y + 1, 2 * CH : 3 * CH, at] = pltpu.roll(v, lanes - zl, 1)

    def put_cz(cz_ref, y, value):
        value = rounded(value)
        cz_ref[y, 0:CH, :] = after(value, hops).astype(bf16)
        cz_ref[y, CH : 2 * CH, :] = tile(value, hops).astype(bf16)
        cz_ref[y, 2 * CH : 3 * CH, :] = before(value, hops).astype(bf16)

    def convolve(src, w, ys):
        sums = []
        for first in range(0, len(ys), 2 * SPAN):
            columns = jnp.concatenate(
                [
                    src[pl.ds(ys[at], SPAN + 2)].reshape((SPAN + 2) * 3 * CH, nt * lanes)
                    for at in range(first, first + 2 * SPAN, SPAN)
                ],
                axis=1,
            )
            results = jnp.dot(w, columns, preferred_element_type=f32)
            for u in range(2 * SPAN):
                at = (u // SPAN) * nt * lanes
                parts = results[
                    (u % SPAN) * 3 * CH : (u % SPAN + 1) * 3 * CH, at : at + nt * lanes
                ]
                low, mid, high = parts[0:CH], parts[CH : 2 * CH], parts[2 * CH :]
                sums.append(
                    jnp.concatenate(
                        [tile(mid, t) + before(low, t) + after(high, t) for t in range(nt)], axis=1
                    )
                )
        return sums

    def rows_at(j):
        return [unroll * j + u for u in range(unroll)]

    return tile, put, put_cz, convolve, rows_at


def stored(far_ref, i, near_ref):
    rows, _, columns = near_ref.shape
    return far_ref.at[i, 0:rows, :, 0:columns]


def forward_kernel(dims, *refs):
    n, hops, groups, _, cy, _, zl, length, unroll = dims
    nt = 2 * hops + 1
    tiles = refs[:nt]
    wf_ref, idx_ref = refs[nt : nt + 2]
    bsend_ref, ssend_ref = refs[nt + 2 : nt + 4]
    far_ref = refs[nt + 4]
    acts = refs[nt + 5 : nt + 9]
    cot_ref, cz_ref, f_ref, fs_ref, sems = refs[nt + 9 :]
    near = (*acts, cot_ref, cz_ref)

    def save(i):
        return pltpu.make_async_copy(near[i], stored(far_ref, i, near[i]), sems.at[i])

    group = tiles[0].shape[1]
    lanes = tiles[0].shape[2]
    tile, put, put_cz, convolve, rows_at = closure_tools(nt, hops, lanes, zl, unroll)

    for ref in (*acts, cot_ref):
        zero = jnp.zeros((3 * CH, nt * lanes), bf16)
        ref[0] = zero
        ref[cy + 1] = zero
    for t in range(nt):
        used = n * group
        if used < CH * cy:
            f_ref[t, used:, :] = jnp.zeros((CH * cy - used, lanes), f32)

        def swap(j, carry, t=t):
            base = pl.multiple_of(16 * j, 16)
            parts = granule_swap([tiles[t][s, pl.ds(base, 16), :].astype(f32) for s in range(n)])
            turn = (t - hops) * zl % lanes
            for r in range(n):
                part = pltpu.roll(parts[r], turn, 1) if turn else parts[r]
                f_ref[t, pl.ds(r * group + base, 16), :] = part
            return carry

        lax.fori_loop(0, group // 16, swap, 0)

    def load_fields(y):
        return jnp.concatenate([f_ref[t, pl.ds(y, CH, stride=cy), :] for t in range(nt)], axis=1)

    def start(j, carry):
        for y in rows_at(j):
            put(acts[0], y, load_fields(y))
        return carry

    lax.fori_loop(0, cy // unroll, start, 0)
    save(0).start()

    for k in range(LAYERS - 1):
        w = wf_ref[k]

        def forward(j, carry, k=k, w=w):
            ys = rows_at(j)
            outs = [jnp.tanh(v) for v in convolve(acts[k], w, ys)]
            for y, v in zip(ys, outs):
                put(acts[k + 1], y, v)
            return carry

        lax.fori_loop(0, cy // unroll, forward, 0)
        save(k + 1).start()

    w_last = wf_ref[LAYERS - 1]
    channel = lax.broadcasted_iota(jnp.int32, (CH, nt * lanes), 0)
    stressed = (channel >= 3) & (channel < 9)

    def predict(j, carry):
        ys = rows_at(j)
        targets = [load_fields(y) for y in ys]
        predicted = convolve(acts[LAYERS - 1], w_last, ys)
        cots = [
            jnp.where(stressed, 2.0 / length * (v - target), 0.0)
            for v, target in zip(predicted, targets)
        ]
        for y, cot in zip(ys, cots):
            put(cot_ref, y, cot)
            put_cz(cz_ref, y, cot)
        for y, v in zip(ys, predicted):
            stress = rounded(v)
            for t in range(nt):
                f_ref[t, pl.ds(y, CH, stride=cy), :] = tile(stress, t)
        return carry

    lax.fori_loop(0, cy // unroll, predict, 0)
    save(LAYERS).start()
    save(LAYERS + 1).start()

    left = jnp.concatenate(
        [
            f_ref[t, (3 + 3 * half) * cy : (6 + 3 * half) * cy, :].astype(bf16)
            for half in range(2)
            for t in range(nt)
        ],
        axis=1,
    )
    row = lax.broadcasted_iota(jnp.int32, (2 * nt * lanes, 256), 0)
    for d in range(n // 2):
        pick = jnp.where(row == idx_ref[d], 1.0, 0.0).astype(bf16)
        moved = jnp.dot(left, pick, preferred_element_type=f32).astype(bf16)
        bsend_ref[2 * d] = moved[:, 0:128]
        bsend_ref[2 * d + 1] = moved[:, 128:256]

    wide = cy // groups
    srows = ssend_ref.shape[1]
    fs_ref[...] = jnp.zeros(fs_ref.shape, f32)
    for g in range(groups):
        for c in range(6):
            at = (3 + c) * cy + g * wide
            fs_ref[c * wide : (c + 1) * wide, :] = f_ref[hops, at : at + wide, :]
        for j in range(srows // 16):
            parts = granule_swap(
                [fs_ref[r * srows + 16 * j : r * srows + 16 * j + 16, :] for r in range(n)]
            )
            for d in range(n):
                ssend_ref[g * n + d, 16 * j : 16 * j + 16, :] = parts[d]
    for i in range(LAYERS + 2):
        save(i).wait()


def backward_kernel(dims, *refs):
    _, hops, _, devices, cy, _, zl, _, unroll = dims
    nt = 2 * hops + 1
    wb_ref, ssend_ref = refs[:2]
    far_ref, sum_ref = refs[2:4]
    acts = refs[4:8]
    cot_ref, cz_in_ref, cz_ref, g_ref, grad_ref, sems = refs[8:]
    near = (*acts, cot_ref, cz_in_ref)

    def fetch(i):
        return pltpu.make_async_copy(stored(far_ref, i, near[i]), near[i], sems.at[i])

    for i in (LAYERS + 1, LAYERS - 1, LAYERS, *range(LAYERS - 2, -1, -1)):
        fetch(i).start()
    lanes = ssend_ref.shape[2]
    own = hops * lanes
    _, put, put_cz, convolve, rows_at = closure_tools(nt, hops, lanes, zl, unroll)

    def weight_gradient(src, cz_ref, k):
        def pair(j, acc):
            ys = [BATCH * j + u for u in range(BATCH)]
            left = jnp.concatenate([cz_ref[y] for y in ys], axis=1)
            right = jnp.concatenate(
                [src[pl.ds(y, 3), :, own : own + lanes].reshape(9 * CH, lanes) for y in ys],
                axis=1,
            )
            return acc + lax.dot_general(
                left, right, (((1,), (1,)), ((), ())), preferred_element_type=f32
            )

        g_ref[k] = lax.fori_loop(0, cy // BATCH, pair, jnp.zeros((3 * CH, 9 * CH), f32))

    fetch(LAYERS + 1).wait()
    fetch(LAYERS - 1).wait()
    weight_gradient(acts[LAYERS - 1], cz_in_ref, LAYERS - 1)
    fetch(LAYERS).wait()
    source = cot_ref
    for k in range(LAYERS - 1, 0, -1):
        w = wb_ref[k]
        here = acts[k]

        def backward(j, carry, w=w, here=here, source=source, k=k):
            ys = rows_at(j)
            below = [here[y + 1, CH : 2 * CH, :].astype(f32) for y in ys]
            cots = [v * (1.0 - b * b) for v, b in zip(convolve(source, w, ys), below)]
            for y, cot in zip(ys, cots):
                if k > 1:
                    put(here, y, cot)
                put_cz(cz_ref, y, cot)
            return carry

        lax.fori_loop(0, cy // unroll, backward, 0)
        fetch(k - 1).wait()
        weight_gradient(acts[k - 1], cz_ref, k - 1)
        source = here

    rows = LAYERS * 3 * CH
    main = 8 * CH
    rest = jnp.zeros((rows // 8, main), f32)
    for k in range(LAYERS):
        grad_ref[k * 3 * CH : (k + 1) * 3 * CH, :] = g_ref[k, :, 0:main]
        for half in range(2):
            j = 2 * k + half
            piece = g_ref[k, half * 24 : half * 24 + 24, main:]
            piece = jnp.concatenate([piece, jnp.zeros((24, main - CH), f32)], axis=1)
            rest = rest + (pltpu.roll(piece, j * CH, 1) if j else piece)
    grad_ref[rows : rows + rows // 8, :] = rest
    if grad_ref.shape[0] > rows + rows // 8:
        grad_ref[rows + rows // 8 :, :] = jnp.zeros(
            (grad_ref.shape[0] - rows - rows // 8, main), f32
        )

    share = grad_ref.shape[0] // devices
    for d in range(devices):
        sum_ref[d, 0:share, :] = grad_ref[d * share : (d + 1) * share, :]
        sum_ref[d, share:, :] = ssend_ref[d]


def stress_kernel(n, groups, zl, recv_ref, out_ref, fs_ref):
    comps, cx, wide, _ = out_ref.shape
    srows = fs_ref.shape[1] // n
    skip = recv_ref.shape[1] - srows
    lanes = recv_ref.shape[2]
    cz = n * zl
    for g in range(groups):
        for j in range(srows // 16):
            parts = granule_swap(
                [
                    recv_ref[g * n + s, skip + 16 * j : skip + 16 * j + 16, :]
                    for s in range(n)
                ]
            )
            for r in range(n):
                fs_ref[g, r * srows + 16 * j : r * srows + 16 * j + 16, :] = parts[r]
    row = lax.broadcasted_iota(jnp.int32, (2 * lanes, 2 * cz), 0)
    col = lax.broadcasted_iota(jnp.int32, (2 * lanes, 2 * cz), 1)
    z = col & (cz - 1)
    need = (col >> log2(cz)) * lanes + (z >> log2(zl)) * (cx * zl) + (z & (zl - 1))
    used = round_up(comps * wide, 8)
    for xi in range(cx):
        pick = jnp.where(row == need + xi * zl, 1.0, 0.0).astype(bf16)
        for pair in range(groups // 2):
            left = jnp.concatenate(
                [fs_ref[2 * pair, 0:used, :], fs_ref[2 * pair + 1, 0:used, :]], axis=1
            ).astype(bf16)
            moved = jnp.dot(left, pick, preferred_element_type=f32)
            for c in range(comps):
                out_ref[c, xi, :, 2 * cz * pair : 2 * cz * (pair + 1)] = moved[
                    c * wide : (c + 1) * wide
                ].astype(bf16)


def unpack_kernel(all_ref, in_ref, mid_a_ref, mid_b_ref, out_ref):
    rows = LAYERS * 3 * CH
    main = 8 * CH
    rest = all_ref[rows : rows + rows // 8, :]
    for k, (ref, first, count, inputs) in enumerate(
        ((in_ref, 0, CH, 3), (mid_a_ref, 0, CH, CH), (mid_b_ref, 0, CH, CH), (out_ref, 3, 6, CH))
    ):
        block = all_ref[k * 3 * CH : (k + 1) * 3 * CH, :]
        tails = []
        for half in range(2):
            j = 2 * k + half
            tails.append(pltpu.roll(rest, main - j * CH, 1) if j else rest)
        tail = jnp.concatenate(tails, axis=0)
        for dy in range(3):
            for dx in range(3):
                at = dy * 3 + dx
                if at == 8:
                    moved = tail
                else:
                    moved = pltpu.roll(block, main - at * CH, 1) if at else block
                for dz in range(3):
                    ref[(dx * 3 + dy) * 3 + dz] = moved[
                        dz * CH + first : dz * CH + first + count, 0:inputs
                    ]


def tendency(ref, x, y0, rows, forcing):
    wide = ref.shape[-1]

    def at(c, dx, dy):
        return ref[c, x + dx, y0 + 8 + dy : y0 + 8 + dy + rows, :]

    centre = [at(c, 0, 0) for c in range(3)]
    results = []
    for i in range(3):
        f0 = centre[i]
        total = None
        for j in range(3):
            if j == 0:
                m2, m1, p1, p2 = (at(i, k, 0) for k in (-2, -1, 1, 2))
            elif j == 1:
                m2, m1, p1, p2 = (at(i, 0, k) for k in (-2, -1, 1, 2))
            else:
                m2, m1, p1, p2 = (pltpu.roll(f0, (-k) % wide, 1) for k in (-2, -1, 1, 2))
            slope = 8.0 * (p1 - m1) - (p2 - m2)
            curve = 16.0 * (p1 + m1) - (p2 + m2) - 30.0 * f0
            term = viscosity * curve - centre[j] * slope
            total = term if total is None else total + term
        results.append((f0, total / 12.0 + forcing[i]))
    return results


def advance_kernel(n, v_ref, ez_ref, xl_ref, xr_ref, st_ref, idx_ref, out_ref, u_ref, f1_ref, t_ref, frc_ref):
    comps, fine_x, fine_y, fine_z = v_ref.shape
    cy = fine_y // 2
    wide = 2 * fine_z
    pad = jnp.zeros((8, wide), f32)
    rows_v = comps * fine_x * fine_y
    for c in range(comps):
        for x in range(3 * fine_x):
            u_ref[c, x, 0:8, :] = pad
            u_ref[c, x, fine_y + 8 : fine_y + 16, :] = pad
        for x in range(fine_x):
            at = slice((c * fine_x + x) * fine_y, (c * fine_x + x + 1) * fine_y)
            u_ref[c, x, 8 : fine_y + 8, 0:fine_z] = xl_ref[at, :].astype(f32)
            u_ref[c, fine_x + x, 8 : fine_y + 8, 0:fine_z] = v_ref[c, x]
            u_ref[c, 2 * fine_x + x, 8 : fine_y + 8, 0:fine_z] = xr_ref[at, :].astype(f32)
        for x in range(2 * fine_x):
            f1_ref[c, x, 0:8, :] = pad
            f1_ref[c, x, fine_y + 8 : fine_y + 16, :] = pad
    edges = jnp.concatenate(
        [
            jnp.concatenate([ref[at : at + fine_y, :], ref[at + fine_y : at + 2 * fine_y, :]], axis=1)
            for ref, at in ((xl_ref, rows_v), (ez_ref, 0), (xr_ref, rows_v))
        ],
        axis=0,
    )
    row = lax.broadcasted_iota(jnp.int32, (256, 2 * fine_z), 0)
    col = lax.broadcasted_iota(jnp.int32, (256, 2 * fine_z), 1)
    lane = col & (fine_z - 1)
    for c in range(comps):
        for x in range(0, fine_x, 2):
            base = (c * fine_x + x) * 8 + (col >> log2(fine_z)) * 8
            need = jnp.where(lane < 4, 128 + base + lane, base + lane - (fine_z - 8))
            hit = (row == need) & ((lane < 4) | (lane >= fine_z - 4))
            moved = jnp.dot(
                edges, jnp.where(hit, 1.0, 0.0).astype(bf16), preferred_element_type=f32
            )
            for s in range(3):
                for e in range(2):
                    u_ref[c, s * fine_x + x + e, 8 : fine_y + 8, fine_z:wide] = moved[
                        s * fine_y : (s + 1) * fine_y, e * fine_z : (e + 1) * fine_z
                    ]

    half_lane = lax.broadcasted_iota(jnp.int32, (3 * cy, 128), 1) < 64
    lows, highs = [], []
    for s in range(0, n, 2):
        a, b = st_ref[s].astype(f32), st_ref[s + 1].astype(f32)
        lows.append(jnp.where(half_lane, a, pltpu.roll(b, 64, 1)).astype(bf16))
        highs.append(jnp.where(half_lane, pltpu.roll(a, 64, 1), b).astype(bf16))
    low = jnp.concatenate(lows, axis=1)
    high = jnp.concatenate(highs, axis=1)
    row = lax.broadcasted_iota(jnp.int32, (64 * n, wide), 0)
    for k in range(6):
        pick = jnp.where(row == idx_ref[k], 1.0, 0.0).astype(bf16)
        for h, src in enumerate((low, high)):
            moved = jnp.dot(src, pick, preferred_element_type=f32)
            for c in range(3):
                t_ref[3 * h + c, k, 0:8, :] = pad
                t_ref[3 * h + c, k, cy + 8 : cy + 16, :] = pad
                t_ref[3 * h + c, k, 8 : cy + 8, :] = moved[c * cy : (c + 1) * cy]

    scale = -closure_weight / 12.0

    def force(kk, carry):
        k = kk + 1
        for y0 in range(0, cy, 8):
            for i in range(3):
                ax, ay, az = pair_table[i]
                tz = t_ref[az, k, y0 + 8 : y0 + 16, :]
                m2, m1, p1, p2 = (pltpu.roll(tz, (-e) % wide, 1) for e in (-2, -1, 1, 2))
                along_z = 8.0 * (p1 - m1) - (p2 - m2)
                m, o, p = (t_ref[ay, k, y0 + 8 + e : y0 + 16 + e, :] for e in (-1, 0, 1))
                even = along_z + (8.0 * o - 7.0 * m - p)
                odd = along_z + (7.0 * p - 8.0 * o + m)
                m, o, p = (t_ref[ax, k + e, y0 + 8 : y0 + 16, :] for e in (-1, 0, 1))
                for px in range(2):
                    along_x = 7.0 * p - 8.0 * o + m if px else 8.0 * o - 7.0 * m - p
                    for py, part in enumerate((even, odd)):
                        value = scale * (along_x + part)
                        for h in range(0, wide, 128):
                            frc_ref[
                                h // 128, i, 2 * kk + px, pl.ds(2 * y0 + py, 8, stride=2), :
                            ] = value[:, h : h + 128]
        return carry

    lax.fori_loop(0, fine_x, force, 0)

    def forcing_at(x, y0):
        return [
            jnp.concatenate(
                [frc_ref[h, i, x, y0 : y0 + rows, :] for h in range(wide // 128)], axis=1
            )
            for i in range(3)
        ]

    rows = 8

    def one(x, carry):
        for y0 in range(0, fine_y, rows):
            for i, (f0, t) in enumerate(tendency(u_ref, x + 2, y0, rows, forcing_at(x, y0))):
                f1_ref[i, x, y0 + 8 : y0 + 8 + rows, :] = f0 + step_size * t
        return carry

    lax.fori_loop(0, 2 * fine_x, one, 0)

    def two(x, carry):
        for y0 in range(0, fine_y, rows):
            for i, (f0, t) in enumerate(tendency(f1_ref, x + 2, y0, rows, forcing_at(x + 2, y0))):
                nxt = (f0 + step_size * t)[:, 0:fine_z]
                out_ref[i, x, y0 : y0 + rows, :] = 0.5 * (v_ref[i, x, y0 : y0 + rows, :] + nxt)
        return carry

    lax.fori_loop(0, fine_x, two, 0)


def send_table(n, hops, cx, zl, lanes):
    nt = 2 * hops + 1
    total_x = n * cx
    window = zl + 2
    table = np.full((2, n // 2, 1, 256), -1, np.int32)
    for variant in range(2):
        z0 = -2 if variant == 0 else 0
        for d in range(n):
            for half in range(2):
                for xk in range(cx + 4):
                    for e in range(window):
                        x = (cx * d - 2 + xk) % total_x
                        z = z0 + e
                        t, zp = hops + z // zl, z % zl
                        turned = (x + t - hops) % total_x
                        src = half * nt * lanes + t * lanes + turned * zl + zp
                        lane = half * 64 + xk * window + e
                        table[variant, d // 2, 0, (d % 2) * 128 + lane] = src
    return table


def spread_table(n, cx, zl, fine_z):
    window = zl + 2
    table = np.full((cx + 4, 1, 2 * fine_z), -1, np.int32)
    for k in range(cx + 4):
        for lane in range(2 * fine_z):
            if lane < fine_z + 4:
                z = lane // 2
            elif lane >= 2 * fine_z - 4:
                z = (lane - 2 * fine_z) // 2
            else:
                continue
            s = min(max(z // zl, 0), n - 1)
            z0 = -2 if s < n // 2 else 0
            table[k, 0, lane] = s * 64 + k * window + (z - s * zl - z0)
    return table


def step(velocity, w_in, w_mid_a, w_mid_b, w_out):
    n = lax.axis_size("slab")
    groups = lax.axis_size("grp")
    devices = n * groups
    comps, fine_x, fine_y, fine_z = velocity.shape
    cx, cy, cz = fine_x // 2, fine_y // 2, fine_z // 2
    zl = cz // n
    lanes = n * cx * zl
    hops = -(-MARGIN // zl)
    nt = 2 * hops + 1
    assert lanes == 128 and fine_z == 128 and cx == 2 and cy % 8 == 0 and (cx + 4) * (zl + 2) <= 64
    length = 6 * n * cx * cy * groups * cz
    both = ("grp", "slab")

    def ring(x, shift):
        return lax.ppermute(x, both, [(i, (i + shift) % devices) for i in range(devices)])

    def shift(x, axis, by):
        count = lax.axis_size(axis)
        return lax.ppermute(x, axis, [(i, (i + by) % count) for i in range(count)])

    spread = jnp.stack(
        [
            jnp.pad(w_in, ((0, 0), (0, 0), (0, CH - 3))),
            w_mid_a,
            w_mid_b,
            jnp.pad(w_out, ((0, 0), (3, CH - 9), (0, 0))),
        ]
    ).reshape(LAYERS, 3, 3, 3, CH, CH)
    w_fwd = jnp.transpose(spread, (0, 3, 4, 2, 1, 5)).reshape(LAYERS, 3 * CH, 9 * CH)
    w_bwd = jnp.transpose(spread[:, ::-1, ::-1, ::-1], (0, 3, 5, 2, 1, 4)).reshape(
        LAYERS, 3 * CH, 9 * CH
    )

    w_fwd, w_bwd = (
        jnp.concatenate(
            [
                jnp.pad(w, ((0, 0), (0, 0), (3 * CH * u, 3 * CH * (SPAN - 1 - u))))
                for u in range(SPAN)
            ],
            axis=1,
        )
        for w in (w_fwd, w_bwd)
    )

    group = round_up(-(-9 * cy // n), 16)
    fields = call(
        functools.partial(filter_kernel, n),
        jax.ShapeDtypeStruct((n, group, lanes), bf16),
        [pltpu.VMEM((9 * cy, cx * fine_z), f32), pltpu.VMEM((n * group, lanes), f32)],
        4_000_000_000,
        1,
    )(velocity)
    mine = lax.all_to_all(fields, "slab", 0, 0, tiled=True)

    v16, edge = call(
        edge_kernel,
        (
            jax.ShapeDtypeStruct((comps * fine_x * fine_y, fine_z), bf16),
            jax.ShapeDtypeStruct((fine_y, 128), bf16),
        ),
        [],
        1_000_000_000,
        1,
    )(velocity)
    from_left = shift(edge, "grp", 1)
    from_right = shift(edge, "grp", -1)
    edges = jnp.concatenate([from_left, from_right], axis=0)

    lower = [ring(mine, k) for k in range(hops, 0, -1)]
    upper = [ring(mine, -k) for k in range(1, hops + 1)]
    pack = jnp.concatenate([v16, edges], axis=0)
    pack, lower, upper = lax.optimization_barrier((pack, lower, upper))
    pack_left = shift(pack, "slab", 1)
    pack_right = shift(pack, "slab", -1)

    place = lax.axis_index("slab")
    tables = send_table(n, hops, cx, zl, lanes)
    send_idx = jnp.where(place < n // 2, tables[0], tables[1])
    srows = round_up(-(-6 * (cy // groups) // n), 16)
    grad_rows = LAYERS * 3 * CH * 9 // 8
    per_device = round_up(-(-grad_rows // devices), 8)
    act = pltpu.VMEM((cy + 2, 3 * CH, nt * lanes), bf16)
    unroll = max(
        u for u in range(1, cy + 1) if cy % u == 0 and u % (2 * SPAN) == 0 and u * nt <= 108
    )
    dims = (n, hops, groups, devices, cy, cx, zl, length, unroll)
    act = ((cy + 2, 3 * CH, nt * lanes), bf16)
    cz_shape = ((cy, 3 * CH, lanes), bf16)
    bsend, ssend, saved = call(
        functools.partial(forward_kernel, dims),
        (
            jax.ShapeDtypeStruct((n, 3 * cy, 128), bf16),
            jax.ShapeDtypeStruct((devices, srows, lanes), f32),
            jax.ShapeDtypeStruct((LAYERS + 2, *act[0]), bf16),
        ),
        [
            *[pltpu.VMEM(*act)] * (LAYERS + 1),
            pltpu.VMEM(*cz_shape),
            pltpu.VMEM((nt, max(CH * cy, n * group), lanes), f32),
            pltpu.VMEM((n * srows, lanes), f32),
            pltpu.SemaphoreType.DMA((LAYERS + 2,)),
        ],
        20_000_000_000,
        nt + 2,
        low=52,
        far_out=1,
    )(*lower, mine, *upper, w_fwd, send_idx)
    to_sum = call(
        functools.partial(backward_kernel, dims),
        jax.ShapeDtypeStruct((devices, per_device + srows, lanes), f32),
        [
            *[pltpu.VMEM(*act)] * (LAYERS + 1),
            pltpu.VMEM(*cz_shape),
            pltpu.VMEM(*cz_shape),
            pltpu.VMEM((LAYERS, 3 * CH, 9 * CH), f32),
            pltpu.VMEM((devices * per_device, lanes), f32),
            pltpu.SemaphoreType.DMA((LAYERS + 2,)),
        ],
        20_000_000_000,
        3,
        low=52,
        far_in=1,
    )(w_bwd, ssend, saved)

    st = lax.all_to_all(bsend, "slab", 0, 0, tiled=True)
    arrived = lax.all_to_all(to_sum, both, 0, 0, tiled=True)
    total = jnp.sum(arrived[:, :per_device], axis=0)
    summed = lax.all_to_all(
        jnp.broadcast_to(total[None], (devices, per_device, 128)), both, 0, 0, tiled=True
    ).reshape(devices * per_device, 128)
    velocity_next = call(
        functools.partial(advance_kernel, n),
        jax.ShapeDtypeStruct(velocity.shape, f32),
        [
            pltpu.VMEM((comps, 3 * fine_x, fine_y + 16, 2 * fine_z), f32),
            pltpu.VMEM((comps, 2 * fine_x, fine_y + 16, 2 * fine_z), f32),
            pltpu.VMEM((6, cx + 4, cy + 16, 2 * fine_z), f32),
            pltpu.VMEM((2 * fine_z // 128, comps, 2 * fine_x, fine_y, 128), f32),
        ],
        15_000_000_000,
        6,
    )(velocity, edges, pack_left, pack_right, st, spread_table(n, cx, zl, fine_z))

    stress = call(
        functools.partial(stress_kernel, n, groups, zl),
        jax.ShapeDtypeStruct((6, cx, cy // groups, groups * cz), bf16),
        [pltpu.VMEM((groups, n * srows, lanes), f32)],
        1_000_000_000,
        1,
    )(arrived)
    grad_in, grad_mid_a, grad_mid_b, grad_out = call(
        unpack_kernel,
        (
            jax.ShapeDtypeStruct((27, CH, 3), f32),
            jax.ShapeDtypeStruct((27, CH, CH), f32),
            jax.ShapeDtypeStruct((27, CH, CH), f32),
            jax.ShapeDtypeStruct((27, 6, CH), f32),
        ),
        [],
        1_000_000_000,
        1,
    )(summed)
    return (velocity_next, stress, grad_in, grad_mid_a, grad_mid_b, grad_out)


def solution(mesh):
    in_specs = (P(None, "slab", None, "grp"), P(), P(), P(), P())
    out_specs = (P(None, "slab", None, "grp"), P(None, "slab", "grp", None), P(), P(), P(), P())
    return jax.shard_map(step, mesh=mesh, in_specs=in_specs, out_specs=out_specs, check_vma=False)
```
